128 devices in a mesh: lat: 16 (over y_lo, z, core), st: 8 (over x, y_hi).
Axes of the slice: x: 4, y: 4 (y_hi: 2, y_lo: 2; y = y_hi * 2 + y_lo), z: 4, core: 2. Of those that a mesh axis runs over, the one named last changes fastest.
Arguments:
- raw_states: bfloat16 [2, 128, 2, 32, 1024], P(None, 'st', None, 'lat'), may hold values from -50 to 50
- levels: int32 [2, 32, 1024], P(None, 'lat'), may hold values from 0 to 7
- phases: int32 [3, 32, 1024], P(None, 'lat'), may hold values from 0 to 7
- window: int32 [128], P('st'), may hold values from 0 to 15
Outputs:
- velocity: float32 [128, 2, 2, 128], P(('lat', 'st'))
- hall: float32 [128], P(('lat', 'st'))
The draws below stay inside these ranges and needn't reach their ends.
All inputs are finite; a program needn't handle non-finite values.
Results may differ from the reference program's by a relative error of at most 0.0064.
Values may be sent and summed in bfloat16 or wider, within the bound.
A program may use at most 64 MiB of HBM per device.

```python
import math
import jax
import jax.numpy as jnp
from jax import lax

S = 128
LY = 1024
ORDER = 6
WINDOWS = 16
LEVELS = 8
PHASES = 8
NX = 32


def draw_raw_states(key, part):
    key_sample = jax.random.fold_in(key, 11)
    key_amplitude = jax.random.fold_in(key, 12)
    sample = jnp.clip(jax.random.normal(key_sample, (2, S, 2, NX, LY), jnp.float32), -5.0, 5.0)
    spread_log = math.log(10.0)
    amplitude = jnp.exp(spread_log * jax.random.uniform(key_amplitude, (1, S, 1, NX, 1), jnp.float32))
    return (sample * amplitude).astype(jnp.bfloat16)


def draw_levels(key, part):
    key_level = jax.random.fold_in(key, 21)
    base_level = jax.random.randint(key_level, (2, NX, LY), 0, LEVELS // 2 + 1)
    column = jnp.arange(NX, dtype=jnp.int32)[None, :, None]
    drawn = base_level + column * (LEVELS // 2 - 1) // NX
    drawn = drawn.at[0, 0, 0].set(0)
    drawn = drawn.at[1, NX - 1, LY - 1].set(LEVELS - 1)
    return drawn.astype(jnp.int32)


def with_ends(values, rng, low, top_value):
    longest = values.shape.index(max(values.shape))
    spots = []
    for shift in (0, 1):
        where = [jax.random.randint(jax.random.fold_in(rng, axis), (), 0, length) for axis, length in enumerate(values.shape)]
        where[longest] = (where[longest] + shift) % values.shape[longest]
        spots.append(tuple(where))
    return values.at[spots[0]].set(low).at[spots[1]].set(top_value)


def block_scale(key, shape, shards, low, high):
    factor_of, own = 1.0, jax.random.fold_in(key, 6)
    for axis_at, blocks in shards:
        steps = jnp.exp(jax.random.uniform(jax.random.fold_in(own, axis_at), (blocks,), jnp.float32, low / len(shards), high / len(shards)))
        factor_of = factor_of * jnp.repeat(steps, shape[axis_at] // blocks).reshape([-1 if axis == axis_at else 1 for axis in range(len(shape))])
    return factor_of


def setup_inputs(seed: int = 0) -> dict:
    keys = jax.random.split(jax.random.key(seed), 5)
    return {
        "raw_states": draw_raw_states(jax.random.fold_in(keys[4], 71), 0),
        "levels": draw_levels(jax.random.fold_in(keys[4], 71), 0),
        "phases": with_ends(jax.random.randint(keys[2], (3, NX, LY), 0, PHASES), jax.random.fold_in(keys[2], 1), 0, PHASES - 1).astype(jnp.int32),
        "window": with_ends(jax.random.randint(keys[3], (S,), 0, WINDOWS), jax.random.fold_in(keys[3], 1), 0, WINDOWS - 1).astype(jnp.int32),
    }


hop_near = 1.0
hop_far = 0.25
level_step = 0.3
stagger = 0.4
spectrum = 6.0
broaden = 0.2
angle_low = 0.5
angle_high = 2.6
half_root = 0.5 * math.sqrt(3.0)
full_root = math.sqrt(3.0)
block_count = 16

def times_complex(coef_real, coef_imag, sample):
    return jnp.stack([coef_real * sample[0] - coef_imag * sample[1], coef_real * sample[1] + coef_imag * sample[0]])

def hop_terms(bond_of):
    cos_zero, sin_zero = bond_of(0, 0, 0)
    cos_one, sin_one = bond_of(1, 0, 0)
    cos_two, sin_two = bond_of(2, 0, 0)
    cos_one_up, sin_one_up = bond_of(1, 0, 1)
    cos_two_up, sin_two_up = bond_of(2, -1, 1)
    target_first = [(1, 0, 0, -hop_near * cos_zero, -hop_near * sin_zero, 0.0, -1.0), (1, 0, -1, -hop_near * cos_one, -hop_near * sin_one, half_root, 0.5), (1, 1, -1, -hop_near * cos_two, -hop_near * sin_two, -half_root, 0.5)]
    target_second = [(0, 0, 0, -hop_near * cos_zero, hop_near * sin_zero, 0.0, 1.0), (0, 0, 1, -hop_near * cos_one_up, hop_near * sin_one_up, -half_root, -0.5), (0, -1, 1, -hop_near * cos_two_up, hop_near * sin_two_up, half_root, -0.5)]
    forward_hops = [(1, 0, -full_root, 0.0), (-1, 1, half_root, -1.5), (0, -1, half_root, 1.5)]
    for source, parity, table in ((0, 1.0, target_first), (1, -1.0, target_second)):
        for shift_x, shift_y, along_x, along_y in forward_hops:
            table.append((source, shift_x, shift_y, 0.0, parity * hop_far, along_x, along_y))
            table.append((source, -shift_x, -shift_y, 0.0, -parity * hop_far, -along_x, -along_y))
    return (target_first, target_second)

def stencil(getter, bond_of, onsite, with_energy, with_velocity):
    tables = hop_terms(bond_of)
    energy_parts, speed_x_parts, speed_y_parts = ([], [], [])
    for target in (0, 1):
        own_value = getter(target, 0, 0)
        energy_sum = onsite[target] * own_value
        speed_x = jnp.zeros_like(own_value)
        speed_y = jnp.zeros_like(own_value)
        for source, shift_x, shift_y, coef_real, coef_imag, along_x, along_y in tables[target]:
            neighbour = getter(source, shift_x, shift_y)
            if with_energy:
                energy_sum = energy_sum + times_complex(coef_real, coef_imag, neighbour)
            if with_velocity:
                if along_x != 0.0:
                    speed_x = speed_x + times_complex(along_x * coef_imag, -along_x * coef_real, neighbour)
                if along_y != 0.0:
                    speed_y = speed_y + times_complex(along_y * coef_imag, -along_y * coef_real, neighbour)
        energy_parts.append(energy_sum)
        speed_x_parts.append(speed_x)
        speed_y_parts.append(speed_y)
    return (jnp.stack(energy_parts, axis=2), jnp.stack(speed_x_parts, axis=2), jnp.stack(speed_y_parts, axis=2))

def filtered(raw_block, coefs, apply_energy):
    previous = raw_block.astype(jnp.float32)
    total = coefs[0] * previous
    current = apply_energy(previous) / spectrum
    total = total + coefs[1] * current
    for degree in range(2, len(coefs)):
        following = 2.0 * (apply_energy(current) / spectrum) - previous
        total = total + coefs[degree] * following
        previous, current = (current, following)
    return total

def roll_getter(field):

    def getter(source, shift_x, shift_y):
        return jnp.roll(field[:, :, source], (-shift_x, -shift_y), axis=(2, 3))
    return getter

def reference(raw_states, levels, phases, window):
    parity = jnp.array([1.0, -1.0], jnp.float32)[:, None, None]
    onsite = level_step * (levels.astype(jnp.float32) - 0.5 * (LEVELS - 1)) + stagger * parity
    angles = phases.astype(jnp.float32) * (2.0 * math.pi / PHASES)
    cos_all = jnp.cos(angles)
    sin_all = jnp.sin(angles)

    def bond_of(which, shift_x, shift_y):
        return (jnp.roll(cos_all[which], (-shift_x, -shift_y), axis=(0, 1)), jnp.roll(sin_all[which], (-shift_x, -shift_y), axis=(0, 1)))
    thetas = angle_low + (angle_high - angle_low) * window.astype(jnp.float32) / (WINDOWS - 1)
    per_block = S // block_count
    raw_blocks = jnp.transpose(raw_states.reshape(2, block_count, per_block, 2, NX, LY), (1, 0, 2, 3, 4, 5))
    theta_blocks = thetas.reshape(block_count, per_block)

    def one_block(inputs):
        raw_block, theta_block = inputs
        coefs = [(1.0 if degree == 0 else 2.0) * jnp.cos(degree * theta_block)[None, :, None, None, None] for degree in range(ORDER + 1)]

        def apply_energy(field):
            return stencil(roll_getter(field), bond_of, onsite, True, False)[0]
        state = filtered(raw_block, coefs, apply_energy)
        image = apply_energy(state)
        numer = lax.optimization_barrier(jnp.sum(state * image, axis=(0, 2, 3, 4)))
        denom = lax.optimization_barrier(jnp.sum(state * state, axis=(0, 2, 3, 4)))
        state_low = state.astype(jnp.bfloat16)
        state_back = lax.optimization_barrier(state_low).astype(jnp.float32)
        outputs = stencil(roll_getter(state_back), bond_of, onsite, False, True)
        return (state_low, outputs[1].astype(jnp.bfloat16), outputs[2].astype(jnp.bfloat16), numer, denom)
    psi_blocks, speed_x_blocks, speed_y_blocks, numer, denom = lax.map(one_block, (raw_blocks, theta_blocks))
    sites = 2 * NX * LY

    def regroup(blocks):
        return jnp.transpose(blocks, (1, 0, 2, 3, 4, 5)).reshape(2, S, sites)
    psi_flat = regroup(psi_blocks)
    speed_x_flat = regroup(speed_x_blocks)
    speed_y_flat = regroup(speed_y_blocks)
    energies = (numer / denom).reshape(S)
    right_side = jnp.concatenate([jnp.concatenate([psi_flat[0], psi_flat[1]], axis=1), jnp.concatenate([psi_flat[1], -psi_flat[0]], axis=1)], axis=0)

    def project(speeds):
        left_side = jnp.concatenate([speeds[0], speeds[1]], axis=1)
        return jnp.dot(left_side, right_side.T, preferred_element_type=jnp.float32).reshape(S, 2, S)
    norm_scale = 1.0 / math.sqrt(2.0 * NX * LY)
    velocity = jnp.stack([project(speed_x_flat), project(speed_y_flat)], axis=1) * norm_scale
    differ = energies[:, None] - energies[None, :]
    weight = differ / (differ * differ + broaden * broaden)
    hall = lax.optimization_barrier(jnp.sum(weight * (velocity[:, 0, 1] * velocity[:, 1, 0] - velocity[:, 0, 0] * velocity[:, 1, 1]), axis=1))
    return (velocity, hall)
```

```python
import functools
import math

import jax
import jax.numpy as jnp
from jax import lax
from jax.experimental import pallas as pl
from jax.experimental.pallas import tpu as pltpu
from jax.sharding import PartitionSpec as P

ORDER = 6
WINDOWS = 16
LEVELS = 8
PHASES = 8
F32 = jnp.float32
BF16 = jnp.bfloat16
MESH = pl.DeviceIdType.MESH

hop_far = 0.25
level_step = 0.3
stagger = 0.4
spectrum = 6.0
broaden = 0.2
angle_low = 0.5
angle_high = 2.6
half_root = 0.5 * math.sqrt(3.0)

unit = 2.0 / spectrum
LAT = 16
ST = 8
NDEV = LAT * ST
LANES = 128
KX = 4
NH = 8

ON_A, ON_B, C0, S0, C1, S1, C2X, S2X, C1Y, S1Y, C2Y, S2Y = range(12)


def y_up(v):
    return pltpu.roll(v, v.shape[1] - 1, 1)


def y_down(v):
    return pltpu.roll(v, 1, 1)


def x_up(get, k):
    return get(k + 1) if k < KX - 1 else pltpu.roll(get(0), 7, 0)


def x_down(get, k):
    return get(k - 1) if k > 0 else pltpu.roll(get(KX - 1), 1, 0)


def mul(cr, ci, ur, ui):
    return cr * ur - ci * ui, cr * ui + ci * ur


def mulc(cr, ci, ur, ui):
    return cr * ur + ci * ui, cr * ui - ci * ur


def eighth_cos(q):
    e = 2.0 - jnp.minimum(q, 8.0 - q)
    r = math.sqrt(0.5)
    cubic = (1.0 - 2.0 * r) / 6.0
    return e * ((r - cubic) + cubic * (e * e))


def build_coefs(tc, co, c2):
    rows = 80 * LAT // 8
    for k in range(KX):
        kk, e = k // 2, k % 2

        def plane(t):
            return jnp.concatenate(
                [tc[pl.ds(kk * 80 + t * 16 + 2 * h + e, 8, stride=rows), :] for h in range(NH)], axis=1
            )

        for t, (cp, sp) in enumerate(((C0, S0), (C1, S1), (0, 1))):
            q = plane(t)
            cosq = -unit * eighth_cos(q)
            qs = q + 6.0
            qs = jnp.where(qs >= 8.0, qs - 8.0, qs)
            sinq = -unit * eighth_cos(qs)
            if t < 2:
                co[cp, k] = cosq
                co[sp, k] = sinq
            else:
                c2[0, k] = cosq
                c2[1, k] = sinq
            if t == 1:
                co[C1Y, k] = y_up(cosq)
                co[S1Y, k] = y_up(sinq)
            if t == 2:
                co[C2Y, k] = y_up(cosq)
                co[S2Y, k] = y_up(sinq)
        for t, dst, par in ((3, ON_A, 1.0), (4, ON_B, -1.0)):
            co[dst, k] = unit * (level_step * (plane(t) - 0.5 * (LEVELS - 1)) + stagger * par)
    for k in range(KX):
        co[C2X, k] = x_down(lambda kk: c2[0, kk], k)
        co[S2X, k] = x_down(lambda kk: c2[1, kk], k)


def apply_h(get, co, k):
    beta = unit * hop_far
    u = [[get(c, s, k) for c in range(2)] for s in range(2)]
    up = [[x_up(functools.partial(get, c, s), k) for c in range(2)] for s in range(2)]
    dn = [[x_down(functools.partial(get, c, s), k) for c in range(2)] for s in range(2)]
    a = [[beta * (up[s][c] - u[s][c]) for c in range(2)] for s in range(2)]
    b = [[beta * (u[s][c] - dn[s][c]) for c in range(2)] for s in range(2)]
    near = mul(co[C0, k], co[S0, k], *u[1])
    r1 = mul(co[C1Y, k], co[S1Y, k], *u[1])
    r2 = mul(co[C2Y, k], co[S2Y, k], *up[1])
    on = co[ON_A, k]
    a_re = on * u[0][0] + near[0] - (a[0][1] + b[0][1]) + y_up(b[0][1]) + y_down(r1[0] + r2[0] + a[0][1])
    a_im = on * u[0][1] + near[1] + (a[0][0] + b[0][0]) - y_up(b[0][0]) + y_down(r1[1] + r2[1] - a[0][0])
    near = mulc(co[C0, k], co[S0, k], *u[0])
    q1 = mulc(co[C1, k], co[S1, k], *u[0])
    q2 = mulc(co[C2X, k], co[S2X, k], *dn[0])
    on = co[ON_B, k]
    b_re = on * u[1][0] + near[0] + (a[1][1] + b[1][1]) + y_up(q1[0] + q2[0] - b[1][1]) - y_down(a[1][1])
    b_im = on * u[1][1] + near[1] - (a[1][0] + b[1][0]) + y_up(q1[1] + q2[1] + b[1][0]) + y_down(a[1][0])
    return [[a_re, a_im], [b_re, b_im]]


def apply_v(get, co, k):
    inv = 1.0 / unit
    hf = hop_far * half_root
    vf = hop_far * 1.5
    u = [[get(c, s, k) for c in range(2)] for s in range(2)]
    up = [[x_up(functools.partial(get, c, s), k) for c in range(2)] for s in range(2)]
    dn = [[x_down(functools.partial(get, c, s), k) for c in range(2)] for s in range(2)]
    n0 = mul(co[C0, k], co[S0, k], *u[1])
    r1 = mul(co[C1Y, k], co[S1Y, k], *u[1])
    r2 = mul(co[C2Y, k], co[S2Y, k], *up[1])
    dif = [(inv * half_root) * (r1[c] - r2[c]) for c in range(2)]
    tot = [(inv * 0.5) * (r1[c] + r2[c]) for c in range(2)]
    rot = [(dif[1], -dif[0]), (tot[1], -tot[0])]
    own = [None, (-inv * n0[1], inv * n0[0])]
    out = [[None, None], [None, None]]
    s = 0
    out[0][s] = [
        -2.0 * hf * (up[s][c] + dn[s][c])
        + y_up(hf * (u[s][c] + dn[s][c]))
        + y_down(rot[0][c] + hf * (u[s][c] + up[s][c]))
        for c in range(2)
    ]
    out[1][s] = [
        own[1][c] + y_up(vf * (u[s][c] - dn[s][c])) + y_down(rot[1][c] + vf * (u[s][c] - up[s][c]))
        for c in range(2)
    ]
    n0 = mulc(co[C0, k], co[S0, k], *u[0])
    q1 = mulc(co[C1, k], co[S1, k], *u[0])
    q2 = mulc(co[C2X, k], co[S2X, k], *dn[0])
    dif = [(inv * half_root) * (q2[c] - q1[c]) for c in range(2)]
    tot = [(-inv * 0.5) * (q1[c] + q2[c]) for c in range(2)]
    rot = [(dif[1], -dif[0]), (tot[1], -tot[0])]
    own = (inv * n0[1], -inv * n0[0])
    s = 1
    out[0][s] = [
        2.0 * hf * (up[s][c] + dn[s][c])
        + y_up(rot[0][c] - hf * (u[s][c] + dn[s][c]))
        - y_down(hf * (u[s][c] + up[s][c]))
        for c in range(2)
    ]
    out[1][s] = [
        own[c] + y_up(rot[1][c] - vf * (u[s][c] - dn[s][c])) - y_down(vf * (u[s][c] - up[s][c]))
        for c in range(2)
    ]
    return out


def kernel(
    raw, phases, levels, window, vel, hall,
    ph_v, lev_v, c_send, c_recv, r_recv, big, tc, co, c2, field, total,
    p_send, p_recv, v_send, v_recv, left, right, part, s_recv, e_send, e_recv, f_send, f_recv,
    in_sem, r_sem, c_sem, p_sem, v_sem, s_sem, e_sem, f_sem,
):
    lat = lax.axis_index("lat")
    st = lax.axis_index("st")
    state = st * LAT + lat
    me = lat * ST + st

    load_ph = pltpu.make_async_copy(phases, ph_v, in_sem.at[0])
    load_lev = pltpu.make_async_copy(levels, lev_v, in_sem.at[1])
    load_ph.start()
    load_lev.start()

    barrier = pltpu.get_barrier_semaphore()

    @pl.loop(1, NDEV)
    def _(i):
        pl.semaphore_signal(
            barrier, inc=1, device_id=((lat + i // ST) % LAT, (st + i) % ST), device_id_type=MESH
        )

    load_ph.wait()
    load_lev.wait()
    c_send[0:3] = ph_v[...].astype(F32).astype(BF16)
    c_send[3:5] = lev_v[...].astype(F32).astype(BF16)
    pl.semaphore_wait(barrier, NDEV - 1)

    @pl.loop(1, LAT)
    def _(i):
        peer = (lat + i) % LAT
        pltpu.make_async_remote_copy(
            c_send, c_recv.at[lat], c_sem.at[0], c_sem.at[1], device_id=(peer, st), device_id_type=MESH
        ).start()
        pltpu.make_async_remote_copy(
            raw.at[:, peer], r_recv.at[lat], r_sem.at[0], r_sem.at[1], device_id=(peer, st), device_id_type=MESH
        ).start()

    pltpu.make_async_copy(c_send, c_recv.at[lat], c_sem.at[1]).start()
    pltpu.make_async_copy(raw.at[:, lat], r_recv.at[lat], r_sem.at[1]).start()

    pltpu.make_async_copy(c_recv, c_recv, c_sem.at[1]).wait()

    @pl.loop(0, LAT)
    def _(d):
        tc[pl.ds(pl.multiple_of(d * 80, 8), 80), :] = c_recv[d].reshape(80, LANES).astype(F32)

    build_coefs(tc, co, c2)

    w = angle_low + (angle_high - angle_low) * jnp.full((8, LANES), window[lat], jnp.int32).astype(F32) / (
        WINDOWS - 1
    )
    cosines = [jnp.ones((8, LANES), F32), jnp.cos(w)]
    for _ in range(2, ORDER + 1):
        cosines.append(2.0 * cosines[1] * cosines[-1] - cosines[-2])

    pltpu.make_async_copy(r_recv, r_recv, r_sem.at[1]).wait()

    @pl.loop(0, LAT)
    def _(d):
        big[pl.ds(pl.multiple_of(d * 64, 8), 64), :] = r_recv[d].reshape(64, LANES).astype(F32)

    def wide(v):
        return jnp.concatenate([v] * NH, axis=1)

    coef = [wide(cosines[0])] + [wide(2.0 * v) for v in cosines[1:]]
    for cs in range(4):
        c, s = cs // 2, cs % 2
        for k in range(KX):
            kk, e = k // 2, k % 2
            v = jnp.concatenate(
                [big[pl.ds(kk * 64 + cs * 16 + 2 * h + e, 8, stride=128), :] for h in range(NH)], axis=1
            )
            field[0, c, s, k] = v

    for degree in range(1, ORDER + 1):
        now, new = (degree - 1) % 2, degree % 2
        get = lambda c, s, k: field[now, c, s, k]
        for k in range(KX):
            out = apply_h(get, co, k)
            for s in range(2):
                for c in range(2):
                    if degree == 1:
                        v = 0.5 * out[s][c]
                        total[c, s, k] = field[0, c, s, k] + coef[1] * v
                    else:
                        v = out[s][c] - field[new, c, s, k]
                        total[c, s, k] = total[c, s, k] + coef[degree] * v
                    field[new, c, s, k] = v

    numer = jnp.zeros((8, NH * LANES), F32)
    denom = jnp.zeros((8, NH * LANES), F32)
    get = lambda c, s, k: total[c, s, k]
    for k in range(KX):
        out = apply_h(get, co, k)
        for s in range(2):
            for c in range(2):
                v = total[c, s, k]
                numer = numer + v * out[s][c]
                denom = denom + v * v
    energy = jnp.sum(numer) / jnp.sum(denom) * (1.0 / unit)
    lane = lax.broadcasted_iota(jnp.int32, (1, LANES), 1)
    e_send[...] = jnp.where(lane == state, jnp.full((1, LANES), energy, F32), 0.0)

    @pl.loop(1, LAT)
    def _(i):
        pltpu.make_async_remote_copy(
            e_send, e_recv.at[lat], e_sem.at[0], e_sem.at[1], device_id=((lat + i) % LAT, st), device_id_type=MESH
        ).start()

    pltpu.make_async_copy(e_send, e_recv.at[lat], e_sem.at[1]).start()

    for k in range(KX):
        kk, e = k // 2, k % 2
        for cs in range(4):
            c, s = cs // 2, cs % 2
            v = total[c, s, k].astype(BF16).astype(F32)
            total[c, s, k] = v
            for h in range(NH):
                big[pl.ds((kk * 8 + h) * 8 + cs * 2 + e, 8, stride=128), :] = v[:, h * LANES : (h + 1) * LANES]

    @pl.loop(0, NDEV // 2)
    def _(i):
        p_send[pl.ds(2 * i, 2)] = big[pl.ds(pl.multiple_of(i * 16, 16), 16), :].astype(BF16).reshape(2, 8, LANES)

    @pl.loop(1, NDEV)
    def _(i):
        pi, hi = (lat + i // ST) % LAT, (st + i) % ST
        pltpu.make_async_remote_copy(
            p_send.at[pi * ST + hi], p_recv.at[state], p_sem.at[0], p_sem.at[1], device_id=(pi, hi), device_id_type=MESH
        ).start()

    pltpu.make_async_copy(p_send.at[me], p_recv.at[state], p_sem.at[1]).start()

    for k in range(KX):
        kk, e = k // 2, k % 2
        out = apply_v(get, co, k)
        for a in range(2):
            for s in range(2):
                for c in range(2):
                    v = out[a][s][c]
                    for h in range(NH):
                        big[pl.ds((kk * 8 + h) * 16 + a * 8 + (c * 2 + s) * 2 + e, 8, stride=256), :] = v[
                            :, h * LANES : (h + 1) * LANES
                        ]

    @pl.loop(0, NDEV)
    def _(i):
        v_send[i] = big[pl.ds(pl.multiple_of(i * 16, 16), 16), :].astype(BF16)

    @pl.loop(1, NDEV)
    def _(i):
        pi, hi = (lat + i // ST) % LAT, (st + i) % ST
        pltpu.make_async_remote_copy(
            v_send.at[pi * ST + hi], v_recv.at[state], v_sem.at[0], v_sem.at[1], device_id=(pi, hi), device_id_type=MESH
        ).start()

    pltpu.make_async_copy(v_send.at[me], v_recv.at[state], v_sem.at[1]).start()

    pltpu.make_async_copy(e_recv, e_recv, e_sem.at[1]).wait()
    f_send[...] = jnp.sum(e_recv[...], axis=0)

    @pl.loop(1, ST)
    def _(i):
        pltpu.make_async_remote_copy(
            f_send, f_recv.at[st], f_sem.at[0], f_sem.at[1], device_id=(lat, (st + i) % ST), device_id_type=MESH
        ).start()

    pltpu.make_async_copy(f_send, f_recv.at[st], f_sem.at[1]).start()

    pltpu.make_async_copy(p_recv, p_recv, p_sem.at[1]).wait()

    @pl.loop(0, NDEV // 2)
    def _(i):
        big[pl.ds(pl.multiple_of(i * 16, 16), 16), :] = p_recv[pl.ds(2 * i, 2)].reshape(16, LANES).astype(F32)

    for j in range(8):
        v = big[pl.ds(j, NDEV, stride=8), :]
        js = (j + 4) % 8
        right[0, :, j * LANES : (j + 1) * LANES] = v.astype(BF16)
        right[1, :, js * LANES : (js + 1) * LANES] = (v if j >= 4 else -v).astype(BF16)

    pltpu.make_async_copy(v_recv, v_recv, v_sem.at[1]).wait()

    @pl.loop(0, NDEV)
    def _(i):
        big[pl.ds(pl.multiple_of(i * 16, 16), 16), :] = v_recv[i].astype(F32)

    for a in range(2):
        for j in range(8):
            left[a, :, j * LANES : (j + 1) * LANES] = big[pl.ds(a * 8 + j, NDEV, stride=16), :].astype(BF16)
    for a in range(2):
        for c in range(2):
            prod = lax.dot_general(left[a], right[c], (((1,), (1,)), ((), ())), preferred_element_type=F32)
            part[:, 2 * a + c, :] = prod

    @pl.loop(1, NDEV)
    def _(i):
        pi, hi = (lat + i // ST) % LAT, (st + i) % ST
        pltpu.make_async_remote_copy(
            part.at[pi * ST + hi], s_recv.at[me], s_sem.at[0], s_sem.at[1], device_id=(pi, hi), device_id_type=MESH
        ).start()

    pltpu.make_async_copy(part.at[me], s_recv.at[me], s_sem.at[1]).start()

    pltpu.make_async_copy(f_recv, f_recv, f_sem.at[1]).wait()
    energies = jnp.sum(f_recv[...], axis=0)
    own = jnp.sum(jnp.where(lane == me, energies, 0.0), axis=1, keepdims=True)
    differ = own - energies
    weight = differ / (differ * differ + broaden * broaden)

    pltpu.make_async_copy(s_recv, s_recv, s_sem.at[1]).wait()
    velocity = jnp.sum(s_recv[...], axis=0) * (1.0 / 256.0)
    vel[...] = velocity
    cross = velocity[1:2] * velocity[2:3] - velocity[0:1] * velocity[3:4]
    hall[...] = jnp.sum(weight * cross, axis=1, keepdims=True)

    pltpu.make_async_copy(c_recv.at[pl.ds(0, LAT - 1)], c_recv.at[pl.ds(0, LAT - 1)], c_sem.at[0]).wait()
    pltpu.make_async_copy(r_recv.at[pl.ds(0, LAT - 1)], r_recv.at[pl.ds(0, LAT - 1)], r_sem.at[0]).wait()
    pltpu.make_async_copy(e_recv.at[pl.ds(0, LAT - 1)], e_recv.at[pl.ds(0, LAT - 1)], e_sem.at[0]).wait()
    pltpu.make_async_copy(f_recv.at[pl.ds(0, ST - 1)], f_recv.at[pl.ds(0, ST - 1)], f_sem.at[0]).wait()
    pltpu.make_async_copy(p_recv.at[pl.ds(0, NDEV - 1)], p_recv.at[pl.ds(0, NDEV - 1)], p_sem.at[0]).wait()
    pltpu.make_async_copy(v_recv.at[pl.ds(0, NDEV - 1)], v_recv.at[pl.ds(0, NDEV - 1)], v_sem.at[0]).wait()
    pltpu.make_async_copy(s_recv.at[pl.ds(0, NDEV - 1)], s_recv.at[pl.ds(0, NDEV - 1)], s_sem.at[0]).wait()


def rows_of(array):
    head = array.shape[:-2]
    array = array.reshape(head + (2, NH, LANES))
    return jnp.swapaxes(array, -3, -2).reshape(head + (2 * NH, LANES))


def local(raw_states, levels, phases, window):
    vm = pltpu.VMEM
    dma = pltpu.SemaphoreType.DMA
    scratch = [
        vm((3, 16, LANES), jnp.int32), vm((2, 16, LANES), jnp.int32),
        vm((5, 16, LANES), BF16), vm((LAT, 5, 16, LANES), BF16),
        vm((LAT, 2, 2, 16, LANES), BF16),
        vm((2048, LANES), F32), vm((80 * LAT, LANES), F32),
        vm((12, KX, 8, NH * LANES), F32), vm((2, KX, 8, NH * LANES), F32),
        vm((2, 2, 2, KX, 8, NH * LANES), F32), vm((2, 2, KX, 8, NH * LANES), F32),
        vm((NDEV, 8, LANES), BF16), vm((NDEV, 8, LANES), BF16),
        vm((NDEV, 16, LANES), BF16), vm((NDEV, 16, LANES), BF16),
        vm((2, NDEV, 1024), BF16), vm((2, NDEV, 1024), BF16),
        vm((NDEV, 4, LANES), F32), vm((NDEV, 4, LANES), F32),
        vm((1, LANES), F32), vm((LAT, 1, LANES), F32),
        vm((1, LANES), F32), vm((ST, 1, LANES), F32),
    ] + [dma((2,))] * 8
    any_spec = pl.BlockSpec(memory_space=pl.ANY)
    velocity, hall = pl.pallas_call(
        kernel,
        out_shape=(jax.ShapeDtypeStruct((4, LANES), F32), jax.ShapeDtypeStruct((1, 1), F32)),
        in_specs=[any_spec, any_spec, any_spec, pl.BlockSpec(memory_space=pltpu.SMEM)],
        out_specs=(pl.BlockSpec(memory_space=pltpu.VMEM), pl.BlockSpec(memory_space=pltpu.VMEM)),
        scratch_shapes=scratch,
        compiler_params=pltpu.CompilerParams(
            collective_id=0, has_side_effects=True, vmem_limit_bytes=48 * 1024 * 1024
        ),
    )(rows_of(raw_states), rows_of(phases), rows_of(levels), window)
    return velocity.reshape(1, 2, 2, LANES), hall.reshape(1)


def solution(mesh):
    in_specs = (
        P(None, "st", None, "lat", None),
        P(None, "lat", None),
        P(None, "lat", None),
        P("st"),
    )
    out_specs = (P(("lat", "st"), None, None, None), P(("lat", "st")))
    return jax.shard_map(local, mesh=mesh, in_specs=in_specs, out_specs=out_specs, check_vma=False)
```

```python
import functools
import itertools
import math

import jax
import jax.numpy as jnp
from jax import lax
from jax.experimental import pallas as pl
from jax.experimental.pallas import tpu as pltpu
from jax.sharding import PartitionSpec as P

ORDER = 6
WINDOWS = 16
LEVELS = 8
PHASES = 8
F32 = jnp.float32
BF16 = jnp.bfloat16
MESH = pl.DeviceIdType.MESH

hop_far = 0.25
level_step = 0.3
stagger = 0.4
spectrum = 6.0
broaden = 0.2
angle_low = 0.5
angle_high = 2.6
half_root = 0.5 * math.sqrt(3.0)

unit = 2.0 / spectrum
LAT = 16
ST = 8
NDEV = LAT * ST
LANES = 128
KX = 4
NH = 8

ON_A, ON_B, C0, S0, C1, S1, C2X, S2X, C1Y, S1Y, C2Y, S2Y = range(12)


def y_up(v):
    return pltpu.roll(v, v.shape[1] - 1, 1)


def y_down(v):
    return pltpu.roll(v, 1, 1)


def x_up(get, k):
    return get(k + 1) if k < KX - 1 else pltpu.roll(get(0), 7, 0)


def x_down(get, k):
    return get(k - 1) if k > 0 else pltpu.roll(get(KX - 1), 1, 0)


def mul(cr, ci, ur, ui):
    return cr * ur - ci * ui, cr * ui + ci * ur


def mulc(cr, ci, ur, ui):
    return cr * ur + ci * ui, cr * ui - ci * ur


def eighth_cos(q):
    e = 2.0 - jnp.minimum(q, 8.0 - q)
    r = math.sqrt(0.5)
    cubic = (1.0 - 2.0 * r) / 6.0
    return e * ((r - cubic) + cubic * (e * e))


def build_coefs(tc, co, c2):
    rows = 80 * LAT // 8
    for k in range(KX):
        kk, e = k // 2, k % 2

        def plane(t):
            return jnp.concatenate(
                [tc[pl.ds(kk * 80 + t * 16 + 2 * h + e, 8, stride=rows), :] for h in range(NH)], axis=1
            )

        for t, (cp, sp) in enumerate(((C0, S0), (C1, S1), (0, 1))):
            q = plane(t)
            cosq = -unit * eighth_cos(q)
            qs = q + 6.0
            qs = jnp.where(qs >= 8.0, qs - 8.0, qs)
            sinq = -unit * eighth_cos(qs)
            if t < 2:
                co[cp, k] = cosq
                co[sp, k] = sinq
            else:
                c2[0, k] = cosq
                c2[1, k] = sinq
            if t == 1:
                co[C1Y, k] = y_up(cosq)
                co[S1Y, k] = y_up(sinq)
            if t == 2:
                co[C2Y, k] = y_up(cosq)
                co[S2Y, k] = y_up(sinq)
        for t, dst, par in ((3, ON_A, 1.0), (4, ON_B, -1.0)):
            co[dst, k] = unit * (level_step * (plane(t) - 0.5 * (LEVELS - 1)) + stagger * par)
    for k in range(KX):
        co[C2X, k] = x_down(lambda kk: c2[0, kk], k)
        co[S2X, k] = x_down(lambda kk: c2[1, kk], k)


def apply_h(get, co, k):
    beta = unit * hop_far
    u = [[get(c, s, k) for c in range(2)] for s in range(2)]
    up = [[x_up(functools.partial(get, c, s), k) for c in range(2)] for s in range(2)]
    dn = [[x_down(functools.partial(get, c, s), k) for c in range(2)] for s in range(2)]
    a = [[beta * (up[s][c] - u[s][c]) for c in range(2)] for s in range(2)]
    b = [[beta * (u[s][c] - dn[s][c]) for c in range(2)] for s in range(2)]
    near = mul(co[C0, k], co[S0, k], *u[1])
    r1 = mul(co[C1Y, k], co[S1Y, k], *u[1])
    r2 = mul(co[C2Y, k], co[S2Y, k], *up[1])
    on = co[ON_A, k]
    a_re = on * u[0][0] + near[0] - (a[0][1] + b[0][1]) + y_up(b[0][1]) + y_down(r1[0] + r2[0] + a[0][1])
    a_im = on * u[0][1] + near[1] + (a[0][0] + b[0][0]) - y_up(b[0][0]) + y_down(r1[1] + r2[1] - a[0][0])
    near = mulc(co[C0, k], co[S0, k], *u[0])
    q1 = mulc(co[C1, k], co[S1, k], *u[0])
    q2 = mulc(co[C2X, k], co[S2X, k], *dn[0])
    on = co[ON_B, k]
    b_re = on * u[1][0] + near[0] + (a[1][1] + b[1][1]) + y_up(q1[0] + q2[0] - b[1][1]) - y_down(a[1][1])
    b_im = on * u[1][1] + near[1] - (a[1][0] + b[1][0]) + y_up(q1[1] + q2[1] + b[1][0]) + y_down(a[1][0])
    return [[a_re, a_im], [b_re, b_im]]


def apply_v(get, co, k):
    inv = 1.0 / unit
    hf = hop_far * half_root
    vf = hop_far * 1.5
    u = [[get(c, s, k) for c in range(2)] for s in range(2)]
    up = [[x_up(functools.partial(get, c, s), k) for c in range(2)] for s in range(2)]
    dn = [[x_down(functools.partial(get, c, s), k) for c in range(2)] for s in range(2)]
    n0 = mul(co[C0, k], co[S0, k], *u[1])
    r1 = mul(co[C1Y, k], co[S1Y, k], *u[1])
    r2 = mul(co[C2Y, k], co[S2Y, k], *up[1])
    dif = [(inv * half_root) * (r1[c] - r2[c]) for c in range(2)]
    tot = [(inv * 0.5) * (r1[c] + r2[c]) for c in range(2)]
    rot = [(dif[1], -dif[0]), (tot[1], -tot[0])]
    own = [None, (-inv * n0[1], inv * n0[0])]
    out = [[None, None], [None, None]]
    s = 0
    out[0][s] = [
        -2.0 * hf * (up[s][c] + dn[s][c])
        + y_up(hf * (u[s][c] + dn[s][c]))
        + y_down(rot[0][c] + hf * (u[s][c] + up[s][c]))
        for c in range(2)
    ]
    out[1][s] = [
        own[1][c] + y_up(vf * (u[s][c] - dn[s][c])) + y_down(rot[1][c] + vf * (u[s][c] - up[s][c]))
        for c in range(2)
    ]
    n0 = mulc(co[C0, k], co[S0, k], *u[0])
    q1 = mulc(co[C1, k], co[S1, k], *u[0])
    q2 = mulc(co[C2X, k], co[S2X, k], *dn[0])
    dif = [(inv * half_root) * (q2[c] - q1[c]) for c in range(2)]
    tot = [(-inv * 0.5) * (q1[c] + q2[c]) for c in range(2)]
    rot = [(dif[1], -dif[0]), (tot[1], -tot[0])]
    own = (inv * n0[1], -inv * n0[0])
    s = 1
    out[0][s] = [
        2.0 * hf * (up[s][c] + dn[s][c])
        + y_up(rot[0][c] - hf * (u[s][c] + dn[s][c]))
        - y_down(hf * (u[s][c] + up[s][c]))
        for c in range(2)
    ]
    out[1][s] = [
        own[c] + y_up(rot[1][c] - vf * (u[s][c] - dn[s][c])) - y_down(vf * (u[s][c] - up[s][c]))
        for c in range(2)
    ]
    return out


def hops(dyl, dz, dx, dyh):
    return (1 if dyl else 2 * dyh) + min(dz, 4 - dz) + min(dx, 4 - dx)


OFFSETS = sorted(itertools.product(range(2), range(4), range(4), range(2)), key=lambda d: (-hops(*d), d))


def chips(lat, st):
    yl, z, x, yh = lat // 8, lax.rem(lat // 2, 4), st // 2, lax.rem(st, 2)
    rows = {(a, b): lax.rem(yl + a, 2) * 8 + lax.rem(z + b, 4) * 2 for a in range(2) for b in range(4)}
    columns = {(a, b): lax.rem(x + a, 4) * 2 + lax.rem(yh + b, 2) for a in range(4) for b in range(2)}
    return [(rows[d[:2]], columns[d[2:]]) for d in OFFSETS if any(d)]


def kernel(
    raw, phases, levels, window, vel, hall,
    ph_v, lev_v, c_send, c_recv, r_recv, big, tc, co, c2, field, total, low,
    m_send, m_recv, left, right, part, s_recv, e_send, e_recv, f_send, f_recv,
    in_sem, r_sem, c_sem, d_sem, m_out, m_in, s_sem, e_sem, f_sem, known,
):
    lat = lax.axis_index("lat")
    st = lax.axis_index("st")
    state = st * LAT + lat
    me = lat * ST + st
    core = lax.rem(lat, 2)
    twin = lat + 1 - 2 * core

    def remote(src, dst, out_sem, in_sem, row, column):
        return pltpu.make_async_remote_copy(
            src, dst, out_sem, in_sem, device_id=(row, column), device_id_type=MESH
        )

    def wait_for(ref, sem):
        pltpu.make_async_copy(ref, ref, sem).wait()

    load_ph = pltpu.make_async_copy(phases, ph_v, in_sem.at[0])
    load_lev = pltpu.make_async_copy(levels, lev_v, in_sem.at[1])
    load_ph.start()
    load_lev.start()
    barrier = pltpu.get_barrier_semaphore()
    for i in range(1, LAT):
        pl.semaphore_signal(barrier, inc=1, device_id=(lax.rem(lat + i, LAT), st), device_id_type=MESH)
    for i in range(1, ST):
        pl.semaphore_signal(barrier, inc=1, device_id=(lat, lax.rem(st + i, ST)), device_id_type=MESH)
    load_ph.wait()
    load_lev.wait()
    c_send[0:3] = ph_v[...].astype(F32).astype(BF16)
    c_send[3:5] = lev_v[...].astype(F32).astype(BF16)
    pl.semaphore_wait(barrier, LAT + ST - 2)

    for i in range(2, LAT, 2):
        remote(c_send, c_recv.at[lat], c_sem.at[0], c_sem.at[1], lax.rem(lat + i, LAT), st).start()
    pltpu.make_async_copy(c_send, c_recv.at[lat], c_sem.at[1]).start()
    for i in range(1, LAT):
        peer = lax.rem(lat + i, LAT)
        remote(raw.at[:, peer], r_recv.at[lat], r_sem.at[0], r_sem.at[1], peer, st).start()
    pltpu.make_async_copy(raw.at[:, lat], r_recv.at[lat], r_sem.at[1]).start()
    for i in range(1, LAT):
        pl.semaphore_signal(known, inc=1, device_id=(lax.rem(lat + i, LAT), st), device_id_type=MESH)

    w = angle_low + (angle_high - angle_low) * jnp.full((8, LANES), window[lat], jnp.int32).astype(F32) / (
        WINDOWS - 1
    )
    cosines = [jnp.ones((8, LANES), F32), jnp.cos(w)]
    for _ in range(2, ORDER + 1):
        cosines.append(2.0 * cosines[1] * cosines[-1] - cosines[-2])

    wait_for(c_recv.at[pl.ds(0, LAT // 2)], c_sem.at[1])
    for i in range(0, LAT, 2):
        row = i + core
        remote(c_recv.at[row], c_recv.at[row], d_sem.at[0], d_sem.at[1], twin, st).start()
    wait_for(c_recv.at[pl.ds(0, LAT // 2)], d_sem.at[1])

    @pl.loop(0, LAT)
    def _(d):
        tc[pl.ds(pl.multiple_of(d * 80, 8), 80), :] = c_recv[d].reshape(80, LANES).astype(F32)

    build_coefs(tc, co, c2)

    wait_for(r_recv, r_sem.at[1])

    @pl.loop(0, LAT)
    def _(d):
        big[pl.ds(pl.multiple_of(d * 64, 8), 64), :] = r_recv[d].reshape(64, LANES).astype(F32)

    def wide(v):
        return jnp.concatenate([v] * NH, axis=1)

    coef = [wide(cosines[0])] + [wide(2.0 * v) for v in cosines[1:]]
    for cs in range(4):
        c, s = cs // 2, cs % 2
        for k in range(KX):
            kk, e = k // 2, k % 2
            v = jnp.concatenate(
                [big[pl.ds(kk * 64 + cs * 16 + 2 * h + e, 8, stride=128), :] for h in range(NH)], axis=1
            )
            field[0, c, s, k] = v

    for degree in range(1, ORDER + 1):
        now, new = (degree - 1) % 2, degree % 2
        get = lambda c, s, k: field[now, c, s, k]
        for k in range(KX):
            out = apply_h(get, co, k)
            for s in range(2):
                for c in range(2):
                    if degree == 1:
                        v = 0.5 * out[s][c]
                        total[c, s, k] = field[0, c, s, k] + coef[1] * v
                    else:
                        v = out[s][c] - field[new, c, s, k]
                        psi = total[c, s, k] + coef[degree] * v
                        total[c, s, k] = psi
                        if degree == ORDER:
                            low[c, s, k] = psi.astype(BF16).astype(F32)
                    if degree < ORDER:
                        field[new, c, s, k] = v

    pl.semaphore_wait(known, LAT - 1)
    far = chips(lat, st)
    get = lambda c, s, k: low[c, s, k]
    for turn in range(2):
        for e in range(2):
            k = 2 * turn + e
            out = apply_v(get, co, k)
            for s in range(2):
                for c in range(2):
                    for f, v in enumerate((low[c, s, k], out[0][s][c], out[1][s][c])):
                        for h in range(NH):
                            big[pl.ds((turn * 8 + h) * 24 + f * 8 + (c * 2 + s) * 2 + e, 8, stride=384), :] = v[
                                :, h * LANES : (h + 1) * LANES
                            ]

        @pl.loop(0, 8)
        def _(i):
            for h in range(NH):
                block = (2 * i + turn) * 8 + h
                m_send[block] = big[pl.ds(pl.multiple_of(block * 24, 8), 24), :].astype(BF16).reshape(3, 8, LANES)

        for row, column in far:
            p = row + turn
            remote(m_send.at[p * ST + column], m_recv.at[state], m_out, m_in.at[st], p, column).start()

        @pl.when(core == turn)
        def _():
            pltpu.make_async_copy(m_send.at[me], m_recv.at[state], m_in.at[st]).start()

        @pl.when(core != turn)
        def _():
            remote(m_send.at[twin * ST + st], m_recv.at[state], m_out, m_in.at[st], twin, st).start()

    numer = jnp.zeros((8, NH * LANES), F32)
    denom = jnp.zeros((8, NH * LANES), F32)
    get = lambda c, s, k: total[c, s, k]
    for k in range(KX):
        out = apply_h(get, co, k)
        for s in range(2):
            for c in range(2):
                v = total[c, s, k]
                numer = numer + v * out[s][c]
                denom = denom + v * v
    energy = jnp.sum(numer) / jnp.sum(denom) * (1.0 / unit)
    lane = lax.broadcasted_iota(jnp.int32, (1, LANES), 1)
    e_send[...] = jnp.where(lane == state, jnp.full((1, LANES), energy, F32), 0.0)
    for i in range(1, LAT):
        remote(e_send, e_recv.at[lat], e_sem.at[0], e_sem.at[1], lax.rem(lat + i, LAT), st).start()
    pltpu.make_async_copy(e_send, e_recv.at[lat], e_sem.at[1]).start()

    @pl.loop(0, ST)
    def _(i):
        group = lax.rem(st + i, ST)
        first = pl.multiple_of(group * LAT, LAT)
        wait_for(m_recv.at[pl.ds(first, LAT)], m_in.at[group])
        for n in range(LAT):
            big[n * 24 : (n + 1) * 24, :] = m_recv[first + n].reshape(24, LANES).astype(F32)
        for j in range(8):
            v = big[pl.ds(j, LAT, stride=24), :]
            js = (j + 4) % 8
            right[0, pl.ds(first, LAT), j * LANES : (j + 1) * LANES] = v.astype(BF16)
            right[1, pl.ds(first, LAT), js * LANES : (js + 1) * LANES] = (v if j >= 4 else -v).astype(BF16)
            for a in range(2):
                v = big[pl.ds(8 + a * 8 + j, LAT, stride=24), :]
                left[a, pl.ds(first, LAT), j * LANES : (j + 1) * LANES] = v.astype(BF16)

    for a in range(2):
        for c in range(2):
            prod = lax.dot_general(left[a], right[c], (((1,), (1,)), ((), ())), preferred_element_type=F32)
            part[:, 2 * a + c, :] = prod

    for row, column in far:
        for c in range(2):
            p = row + c
            remote(part.at[p * ST + column], s_recv.at[me], s_sem.at[0], s_sem.at[1], p, column).start()
    remote(part.at[twin * ST + st], s_recv.at[me], s_sem.at[0], s_sem.at[1], twin, st).start()
    pltpu.make_async_copy(part.at[me], s_recv.at[me], s_sem.at[1]).start()

    wait_for(e_recv, e_sem.at[1])
    f_send[...] = jnp.sum(e_recv[...], axis=0)
    for i in range(1, ST):
        remote(f_send, f_recv.at[st], f_sem.at[0], f_sem.at[1], lat, lax.rem(st + i, ST)).start()
    pltpu.make_async_copy(f_send, f_recv.at[st], f_sem.at[1]).start()

    wait_for(f_recv, f_sem.at[1])
    energies = jnp.sum(f_recv[...], axis=0)
    own = jnp.sum(jnp.where(lane == me, energies, 0.0), axis=1, keepdims=True)
    differ = own - energies
    weight = differ / (differ * differ + broaden * broaden)

    wait_for(s_recv, s_sem.at[1])

    velocity = jnp.sum(s_recv[...], axis=0) * (1.0 / 256.0)
    vel[...] = velocity.reshape(2, 2, LANES)
    cross = velocity[1:2] * velocity[2:3] - velocity[0:1] * velocity[3:4]
    hall[...] = jnp.sum(weight * cross, axis=1, keepdims=True)

    wait_for(c_recv.at[pl.ds(0, LAT // 2 - 1)], c_sem.at[0])
    wait_for(c_recv.at[pl.ds(0, LAT // 2)], d_sem.at[0])
    wait_for(r_recv.at[pl.ds(0, LAT - 1)], r_sem.at[0])
    wait_for(e_recv.at[pl.ds(0, LAT - 1)], e_sem.at[0])
    wait_for(f_recv.at[pl.ds(0, ST - 1)], f_sem.at[0])
    wait_for(m_recv.at[pl.ds(0, NDEV - 1)], m_out)
    wait_for(s_recv.at[pl.ds(0, NDEV - 1)], s_sem.at[0])


def rows_of(array):
    head = array.shape[:-2]
    array = array.reshape(head + (2, NH, LANES))
    return jnp.swapaxes(array, -3, -2).reshape(head + (2 * NH, LANES))


def local(raw_states, levels, phases, window):
    vm = pltpu.VMEM
    dma = pltpu.SemaphoreType.DMA
    scratch = [
        vm((3, 16, LANES), jnp.int32), vm((2, 16, LANES), jnp.int32),
        vm((5, 16, LANES), BF16), vm((LAT, 5, 16, LANES), BF16),
        vm((LAT, 2, 2, 16, LANES), BF16),
        vm((3072, LANES), F32), vm((80 * LAT, LANES), F32),
        vm((12, KX, 8, NH * LANES), F32), vm((2, KX, 8, NH * LANES), F32),
        vm((2, 2, 2, KX, 8, NH * LANES), F32), vm((2, 2, KX, 8, NH * LANES), F32),
        vm((2, 2, KX, 8, NH * LANES), F32),
        vm((NDEV, 3, 8, LANES), BF16), vm((NDEV, 3, 8, LANES), BF16),
        vm((2, NDEV, 1024), BF16), vm((2, NDEV, 1024), BF16),
        vm((NDEV, 4, LANES), F32), vm((NDEV, 4, LANES), F32),
        vm((1, LANES), F32), vm((LAT, 1, LANES), F32),
        vm((1, LANES), F32), vm((ST, 1, LANES), F32),
        dma((2,)), dma((2,)), dma((2,)), dma((2,)), dma, dma((ST,)), dma((2,)), dma((2,)), dma((2,)),
        pltpu.SemaphoreType.REGULAR,
    ]
    hbm = pl.BlockSpec(memory_space=pltpu.HBM)
    velocity, hall = pl.pallas_call(
        kernel,
        out_shape=(jax.ShapeDtypeStruct((2, 2, LANES), F32), jax.ShapeDtypeStruct((1, 1), F32)),
        in_specs=[hbm, hbm, hbm, pl.BlockSpec(memory_space=pltpu.SMEM)],
        out_specs=(pl.BlockSpec(memory_space=pltpu.VMEM), pl.BlockSpec(memory_space=pltpu.VMEM)),
        scratch_shapes=scratch,
        compiler_params=pltpu.CompilerParams(
            collective_id=0, has_side_effects=True, vmem_limit_bytes=60000000
        ),
    )(rows_of(raw_states), rows_of(phases), rows_of(levels), window)
    return velocity.reshape(1, 2, 2, LANES), hall.reshape(1)


def solution(mesh):
    in_specs = (
        P(None, "st", None, "lat", None),
        P(None, "lat", None),
        P(None, "lat", None),
        P("st"),
    )
    out_specs = (P(("lat", "st"), None, None, None), P(("lat", "st")))
    return jax.shard_map(local, mesh=mesh, in_specs=in_specs, out_specs=out_specs, check_vma=False)
```

```python
import functools
import itertools
import math

import jax
import jax.numpy as jnp
from jax import lax
from jax.experimental import pallas as pl
from jax.experimental.pallas import tpu as pltpu
from jax.sharding import PartitionSpec as P

ORDER = 6
WINDOWS = 16
LEVELS = 8
PHASES = 8
F32 = jnp.float32
BF16 = jnp.bfloat16
MESH = pl.DeviceIdType.MESH

hop_far = 0.25
level_step = 0.3
stagger = 0.4
spectrum = 6.0
broaden = 0.2
angle_low = 0.5
angle_high = 2.6
half_root = 0.5 * math.sqrt(3.0)

unit = 2.0 / spectrum
LAT = 16
ST = 8
NDEV = LAT * ST
LANES = 128
KX = 4
NH = 8

ON_A, ON_B, C0, S0, C1, S1, C2X, S2X, C1Y, S1Y, C2Y, S2Y = range(12)


def y_up(v):
    return pltpu.roll(v, v.shape[1] - 1, 1)


def y_down(v):
    return pltpu.roll(v, 1, 1)


def x_up(get, k):
    return get(k + 1) if k < KX - 1 else pltpu.roll(get(0), 7, 0)


def x_down(get, k):
    return get(k - 1) if k > 0 else pltpu.roll(get(KX - 1), 1, 0)


def mul(cr, ci, ur, ui):
    return cr * ur - ci * ui, cr * ui + ci * ur


def mulc(cr, ci, ur, ui):
    return cr * ur + ci * ui, cr * ui - ci * ur


def eighth_cos(q):
    e = 2.0 - jnp.minimum(q, 8.0 - q)
    r = math.sqrt(0.5)
    cubic = (1.0 - 2.0 * r) / 6.0
    return e * ((r - cubic) + cubic * (e * e))


def build_coefs(tc, co, c2):
    rows = 80 * LAT // 8
    for k in range(KX):
        kk, e = k // 2, k % 2

        def plane(t):
            return jnp.concatenate(
                [tc[pl.ds(kk * 80 + t * 16 + 2 * h + e, 8, stride=rows), :] for h in range(NH)], axis=1
            )

        for t, (cp, sp) in enumerate(((C0, S0), (C1, S1), (0, 1))):
            q = plane(t)
            cosq = -unit * eighth_cos(q)
            qs = q + 6.0
            qs = jnp.where(qs >= 8.0, qs - 8.0, qs)
            sinq = -unit * eighth_cos(qs)
            if t < 2:
                co[cp, k] = cosq
                co[sp, k] = sinq
            else:
                c2[0, k] = cosq
                c2[1, k] = sinq
            if t == 1:
                co[C1Y, k] = y_up(cosq)
                co[S1Y, k] = y_up(sinq)
            if t == 2:
                co[C2Y, k] = y_up(cosq)
                co[S2Y, k] = y_up(sinq)
        for t, dst, par in ((3, ON_A, 1.0), (4, ON_B, -1.0)):
            co[dst, k] = unit * (level_step * (plane(t) - 0.5 * (LEVELS - 1)) + stagger * par)
    for k in range(KX):
        co[C2X, k] = x_down(lambda kk: c2[0, kk], k)
        co[S2X, k] = x_down(lambda kk: c2[1, kk], k)


def apply_h(get, co, k):
    beta = unit * hop_far
    u = [[get(c, s, k) for c in range(2)] for s in range(2)]
    up = [[x_up(functools.partial(get, c, s), k) for c in range(2)] for s in range(2)]
    dn = [[x_down(functools.partial(get, c, s), k) for c in range(2)] for s in range(2)]
    a = [[beta * (up[s][c] - u[s][c]) for c in range(2)] for s in range(2)]
    b = [[beta * (u[s][c] - dn[s][c]) for c in range(2)] for s in range(2)]
    near = mul(co[C0, k], co[S0, k], *u[1])
    r1 = mul(co[C1Y, k], co[S1Y, k], *u[1])
    r2 = mul(co[C2Y, k], co[S2Y, k], *up[1])
    on = co[ON_A, k]
    a_re = on * u[0][0] + near[0] - (a[0][1] + b[0][1]) + y_up(b[0][1]) + y_down(r1[0] + r2[0] + a[0][1])
    a_im = on * u[0][1] + near[1] + (a[0][0] + b[0][0]) - y_up(b[0][0]) + y_down(r1[1] + r2[1] - a[0][0])
    near = mulc(co[C0, k], co[S0, k], *u[0])
    q1 = mulc(co[C1, k], co[S1, k], *u[0])
    q2 = mulc(co[C2X, k], co[S2X, k], *dn[0])
    on = co[ON_B, k]
    b_re = on * u[1][0] + near[0] + (a[1][1] + b[1][1]) + y_up(q1[0] + q2[0] - b[1][1]) - y_down(a[1][1])
    b_im = on * u[1][1] + near[1] - (a[1][0] + b[1][0]) + y_up(q1[1] + q2[1] + b[1][0]) + y_down(a[1][0])
    return [[a_re, a_im], [b_re, b_im]]


def apply_v(get, co, k):
    inv = 1.0 / unit
    hf = hop_far * half_root
    vf = hop_far * 1.5
    u = [[get(c, s, k) for c in range(2)] for s in range(2)]
    up = [[x_up(functools.partial(get, c, s), k) for c in range(2)] for s in range(2)]
    dn = [[x_down(functools.partial(get, c, s), k) for c in range(2)] for s in range(2)]
    n0 = mul(co[C0, k], co[S0, k], *u[1])
    r1 = mul(co[C1Y, k], co[S1Y, k], *u[1])
    r2 = mul(co[C2Y, k], co[S2Y, k], *up[1])
    dif = [(inv * half_root) * (r1[c] - r2[c]) for c in range(2)]
    tot = [(inv * 0.5) * (r1[c] + r2[c]) for c in range(2)]
    rot = [(dif[1], -dif[0]), (tot[1], -tot[0])]
    own = [None, (-inv * n0[1], inv * n0[0])]
    out = [[None, None], [None, None]]
    s = 0
    out[0][s] = [
        -2.0 * hf * (up[s][c] + dn[s][c])
        + y_up(hf * (u[s][c] + dn[s][c]))
        + y_down(rot[0][c] + hf * (u[s][c] + up[s][c]))
        for c in range(2)
    ]
    out[1][s] = [
        own[1][c] + y_up(vf * (u[s][c] - dn[s][c])) + y_down(rot[1][c] + vf * (u[s][c] - up[s][c]))
        for c in range(2)
    ]
    n0 = mulc(co[C0, k], co[S0, k], *u[0])
    q1 = mulc(co[C1, k], co[S1, k], *u[0])
    q2 = mulc(co[C2X, k], co[S2X, k], *dn[0])
    dif = [(inv * half_root) * (q2[c] - q1[c]) for c in range(2)]
    tot = [(-inv * 0.5) * (q1[c] + q2[c]) for c in range(2)]
    rot = [(dif[1], -dif[0]), (tot[1], -tot[0])]
    own = (inv * n0[1], -inv * n0[0])
    s = 1
    out[0][s] = [
        2.0 * hf * (up[s][c] + dn[s][c])
        + y_up(rot[0][c] - hf * (u[s][c] + dn[s][c]))
        - y_down(hf * (u[s][c] + up[s][c]))
        for c in range(2)
    ]
    out[1][s] = [
        own[c] + y_up(rot[1][c] - vf * (u[s][c] - dn[s][c])) - y_down(vf * (u[s][c] - up[s][c]))
        for c in range(2)
    ]
    return out


def hops(dyl, dz, dx, dyh):
    return (1 if dyl else 2 * dyh) + min(dz, 4 - dz) + min(dx, 4 - dx)


OFFSETS = sorted(itertools.product(range(2), range(4), range(4), range(2)), key=lambda d: (-hops(*d), d))


def columns_of_chips(lat):
    yl, z = lat // 8, lax.rem(lat // 2, 4)
    offsets = [(1, 2), (0, 2), (1, 1), (1, 3), (0, 1), (0, 3), (1, 0)]
    return [lax.rem(yl + a, 2) * 8 + lax.rem(z + b, 4) * 2 for a, b in offsets]


def chips(lat, st):
    yl, z, x, yh = lat // 8, lax.rem(lat // 2, 4), st // 2, lax.rem(st, 2)
    rows = {(a, b): lax.rem(yl + a, 2) * 8 + lax.rem(z + b, 4) * 2 for a in range(2) for b in range(4)}
    columns = {(a, b): lax.rem(x + a, 4) * 2 + lax.rem(yh + b, 2) for a in range(4) for b in range(2)}
    return [(rows[d[:2]], columns[d[2:]]) for d in OFFSETS if any(d)]


def kernel(
    raw, phases, levels, window, both,
    win_s, ph_v, lev_v, c_send, c_recv, r_recv, big, tc, co, c2, field, total, low,
    m_send, m_recv, left, right, part, s_recv, e_send, e_recv, f_send, f_recv,
    in_sem, r_sem, c_sem, c_in, d_sem, m_out, m_in, s_sem, e_sem, f_sem, known,
):
    lat = lax.axis_index("lat")
    st = lax.axis_index("st")
    state = st * LAT + lat
    me = lat * ST + st
    core = lax.rem(lat, 2)
    twin = lat + 1 - 2 * core

    def remote(src, dst, out_sem, in_sem, row, column):
        return pltpu.make_async_remote_copy(
            src, dst, out_sem, in_sem, device_id=(row, column), device_id_type=MESH
        )

    def wait_for(ref, sem):
        pltpu.make_async_copy(ref, ref, sem).wait()

    load_ph = pltpu.make_async_copy(phases, ph_v, in_sem.at[0])
    load_lev = pltpu.make_async_copy(levels, lev_v, in_sem.at[1])
    load_win = pltpu.make_async_copy(window, win_s, in_sem.at[2])
    load_ph.start()
    load_lev.start()
    load_win.start()
    near = columns_of_chips(lat)
    x, yh = st // 2, lax.rem(st, 2)
    along = [lax.rem(x + i, 4) * 2 + yh for i in (1, 3)]
    across = (lax.rem(lat + 8, LAT), st + 1 - 2 * yh)

    def greet(sem, row, column):
        pl.semaphore_signal(sem, inc=1, device_id=(row, column), device_id_type=MESH)

    barrier = pltpu.get_barrier_semaphore()
    for row in near:
        greet(barrier, row, st)
        greet(barrier, row + 1, st)
    for column in along:
        greet(barrier, lat, column)
    greet(barrier, *across)
    greet(barrier, twin, st)
    load_ph.wait()
    load_lev.wait()
    load_win.wait()
    c_send[0:3] = ph_v[...].astype(F32).astype(BF16)
    c_send[3:5] = lev_v[...].astype(F32).astype(BF16)
    pl.semaphore_wait(barrier, LAT - 1 + 3)

    mine = lat // 2
    for row in near:
        remote(c_send, c_recv.at[lat], c_sem.at[0], c_in.at[mine], row + core, st).start()
    remote(c_send, c_recv.at[lat], d_sem.at[0], d_sem.at[1], twin, st).start()
    pltpu.make_async_copy(c_send, c_recv.at[lat], c_sem.at[1]).start()
    for row in near:
        for c in range(2):
            remote(raw.at[:, row + c], r_recv.at[lat], r_sem.at[0], r_sem.at[1], row + c, st).start()
    remote(raw.at[:, twin], r_recv.at[lat], r_sem.at[0], r_sem.at[1], twin, st).start()
    pltpu.make_async_copy(raw.at[:, lat], r_recv.at[lat], r_sem.at[1]).start()
    for row in near:
        greet(known.at[0], row, st)
        greet(known.at[0], row + 1, st)
    greet(known.at[0], twin, st)

    w = angle_low + (angle_high - angle_low) * jnp.full((8, LANES), win_s[lat], jnp.int32).astype(F32) / (
        WINDOWS - 1
    )
    cosines = [jnp.ones((8, LANES), F32), jnp.cos(w)]
    for _ in range(2, ORDER + 1):
        cosines.append(2.0 * cosines[1] * cosines[-1] - cosines[-2])

    for row in reversed(near):
        row = row + core
        wait_for(c_recv.at[row], c_in.at[row // 2])
        remote(c_recv.at[row], c_recv.at[row], d_sem.at[0], d_sem.at[1], twin, st).start()
    pl.semaphore_wait(known.at[0], LAT - 1)
    for column in along:
        greet(known.at[1], lat, column)
    wait_for(c_recv.at[lat], c_sem.at[1])
    wait_for(c_recv.at[pl.ds(0, LAT // 2)], d_sem.at[1])

    @pl.loop(0, LAT)
    def _(d):
        tc[pl.ds(pl.multiple_of(d * 80, 8), 80), :] = c_recv[d].reshape(80, LANES).astype(F32)

    build_coefs(tc, co, c2)

    pl.semaphore_wait(known.at[1], 2)
    for column in along:
        greet(known.at[2], lat, column)
    wait_for(r_recv, r_sem.at[1])

    @pl.loop(0, LAT)
    def _(d):
        big[pl.ds(pl.multiple_of(d * 64, 8), 64), :] = r_recv[d].reshape(64, LANES).astype(F32)

    def wide(v):
        return jnp.concatenate([v] * NH, axis=1)

    coef = [wide(cosines[0])] + [wide(2.0 * v) for v in cosines[1:]]
    for cs in range(4):
        c, s = cs // 2, cs % 2
        for k in range(KX):
            kk, e = k // 2, k % 2
            v = jnp.concatenate(
                [big[pl.ds(kk * 64 + cs * 16 + 2 * h + e, 8, stride=128), :] for h in range(NH)], axis=1
            )
            field[0, c, s, k] = v

    for degree in range(1, ORDER + 1):
        now, new = (degree - 1) % 2, degree % 2
        get = lambda c, s, k: field[now, c, s, k]
        for k in range(KX):
            out = apply_h(get, co, k)
            for s in range(2):
                for c in range(2):
                    if degree == 1:
                        v = 0.5 * out[s][c]
                        total[c, s, k] = field[0, c, s, k] + coef[1] * v
                    else:
                        v = out[s][c] - field[new, c, s, k]
                        psi = total[c, s, k] + coef[degree] * v
                        total[c, s, k] = psi
                        if degree == ORDER:
                            low[c, s, k] = psi.astype(BF16).astype(F32)
                    if degree < ORDER:
                        field[new, c, s, k] = v

    pl.semaphore_wait(known.at[2], 2)
    far = chips(lat, st)
    get = lambda c, s, k: low[c, s, k]
    for turn in range(2):
        for e in range(2):
            k = 2 * turn + e
            out = apply_v(get, co, k)
            for s in range(2):
                for c in range(2):
                    for f, v in enumerate((low[c, s, k], out[0][s][c], out[1][s][c])):
                        for h in range(NH):
                            big[pl.ds((turn * 8 + h) * 24 + f * 8 + (c * 2 + s) * 2 + e, 8, stride=384), :] = v[
                                :, h * LANES : (h + 1) * LANES
                            ]

        @pl.loop(0, 8)
        def _(i):
            for h in range(NH):
                block = (2 * i + turn) * 8 + h
                m_send[block] = big[pl.ds(pl.multiple_of(block * 24, 8), 24), :].astype(BF16).reshape(3, 8, LANES)

        for row, column in far:
            p = row + turn
            remote(m_send.at[p * ST + column], m_recv.at[state], m_out, m_in.at[st], p, column).start()

        @pl.when(core == turn)
        def _():
            pltpu.make_async_copy(m_send.at[me], m_recv.at[state], m_in.at[st]).start()

        @pl.when(core != turn)
        def _():
            remote(m_send.at[twin * ST + st], m_recv.at[state], m_out, m_in.at[st], twin, st).start()

    numer = jnp.zeros((8, NH * LANES), F32)
    denom = jnp.zeros((8, NH * LANES), F32)
    get = lambda c, s, k: total[c, s, k]
    for k in range(KX):
        out = apply_h(get, co, k)
        for s in range(2):
            for c in range(2):
                v = total[c, s, k]
                numer = numer + v * out[s][c]
                denom = denom + v * v
    energy = jnp.sum(numer) / jnp.sum(denom) * (1.0 / unit)
    lane = lax.broadcasted_iota(jnp.int32, (1, LANES), 1)
    e_send[...] = jnp.where(lane == state, jnp.full((1, LANES), energy, F32), 0.0)
    for i in range(1, LAT):
        remote(e_send, e_recv.at[lat], e_sem.at[0], e_sem.at[1], lax.rem(lat + i, LAT), st).start()
    pltpu.make_async_copy(e_send, e_recv.at[lat], e_sem.at[1]).start()

    @pl.loop(0, ST)
    def _(i):
        group = lax.rem(st + i, ST)
        first = pl.multiple_of(group * LAT, LAT)
        wait_for(m_recv.at[pl.ds(first, LAT)], m_in.at[group])
        for n in range(LAT):
            big[n * 24 : (n + 1) * 24, :] = m_recv[first + n].reshape(24, LANES).astype(F32)
        for j in range(8):
            v = big[pl.ds(j, LAT, stride=24), :]
            js = (j + 4) % 8
            right[0, pl.ds(first, LAT), j * LANES : (j + 1) * LANES] = v.astype(BF16)
            right[1, pl.ds(first, LAT), js * LANES : (js + 1) * LANES] = (v if j >= 4 else -v).astype(BF16)
            for a in range(2):
                v = big[pl.ds(8 + a * 8 + j, LAT, stride=24), :]
                left[a, pl.ds(first, LAT), j * LANES : (j + 1) * LANES] = v.astype(BF16)

    for a in range(2):
        for c in range(2):
            prod = lax.dot_general(left[a], right[c], (((1,), (1,)), ((), ())), preferred_element_type=F32)
            part[:, 2 * a + c, :] = prod

    for row, column in far:
        for c in range(2):
            p = row + c
            remote(part.at[p * ST + column], s_recv.at[me], s_sem.at[0], s_sem.at[1], p, column).start()
    remote(part.at[twin * ST + st], s_recv.at[me], s_sem.at[0], s_sem.at[1], twin, st).start()
    pltpu.make_async_copy(part.at[me], s_recv.at[me], s_sem.at[1]).start()

    wait_for(e_recv, e_sem.at[1])
    f_send[...] = jnp.sum(e_recv[...], axis=0)
    for i in range(1, ST):
        remote(f_send, f_recv.at[st], f_sem.at[0], f_sem.at[1], lat, lax.rem(st + i, ST)).start()
    pltpu.make_async_copy(f_send, f_recv.at[st], f_sem.at[1]).start()

    wait_for(f_recv, f_sem.at[1])
    energies = jnp.sum(f_recv[...], axis=0)
    own = jnp.sum(jnp.where(lane == me, energies, 0.0), axis=1, keepdims=True)
    differ = own - energies
    weight = differ / (differ * differ + broaden * broaden)

    wait_for(s_recv, s_sem.at[1])

    sums = jnp.sum(s_recv[...], axis=0)
    velocity = sums * (1.0 / 256.0)
    both[0:4] = sums
    cross = velocity[1:2] * velocity[2:3] - velocity[0:1] * velocity[3:4]
    both[4:5] = jnp.broadcast_to(jnp.sum(weight * cross, axis=1, keepdims=True), (1, LANES))

    wait_for(c_recv.at[pl.ds(0, LAT // 2 - 1)], c_sem.at[0])
    wait_for(c_recv.at[pl.ds(0, LAT // 2)], d_sem.at[0])
    wait_for(r_recv.at[pl.ds(0, LAT - 1)], r_sem.at[0])
    wait_for(e_recv.at[pl.ds(0, LAT - 1)], e_sem.at[0])
    wait_for(f_recv.at[pl.ds(0, ST - 1)], f_sem.at[0])
    wait_for(m_recv.at[pl.ds(0, NDEV - 1)], m_out)
    wait_for(s_recv.at[pl.ds(0, NDEV - 1)], s_sem.at[0])


def rows_of(array):
    head = array.shape[:-2]
    array = array.reshape(head + (2, NH, LANES))
    return jnp.swapaxes(array, -3, -2).reshape(head + (2 * NH, LANES))


def local(raw_states, levels, phases, window):
    vm = pltpu.VMEM
    dma = pltpu.SemaphoreType.DMA
    scratch = [
        pltpu.SMEM((LAT,), jnp.int32),
        vm((3, 16, LANES), jnp.int32), vm((2, 16, LANES), jnp.int32),
        vm((5, 16, LANES), BF16), vm((LAT, 5, 16, LANES), BF16),
        vm((LAT, 2, 2, 16, LANES), BF16),
        vm((3072, LANES), F32), vm((80 * LAT, LANES), F32),
        vm((12, KX, 8, NH * LANES), F32), vm((2, KX, 8, NH * LANES), F32),
        vm((2, 2, 2, KX, 8, NH * LANES), F32), vm((2, 2, KX, 8, NH * LANES), F32),
        vm((2, 2, KX, 8, NH * LANES), F32),
        vm((NDEV, 3, 8, LANES), BF16), vm((NDEV, 3, 8, LANES), BF16),
        vm((2, NDEV, 1024), BF16), vm((2, NDEV, 1024), BF16),
        vm((NDEV, 4, LANES), F32), vm((NDEV, 4, LANES), F32),
        vm((1, LANES), F32), vm((LAT, 1, LANES), F32),
        vm((1, LANES), F32), vm((ST, 1, LANES), F32),
        dma((3,)), dma((2,)), dma((2,)), dma((LAT // 2,)), dma((2,)), dma, dma((ST,)), dma((2,)), dma((2,)), dma((2,)),
        pltpu.SemaphoreType.REGULAR((3,)),
    ]
    hbm = pl.BlockSpec(memory_space=pltpu.HBM)
    both = pl.pallas_call(
        kernel,
        out_shape=jax.ShapeDtypeStruct((8, LANES), F32),
        in_specs=[hbm] * 4,
        out_specs=pl.BlockSpec(memory_space=pltpu.VMEM),
        scratch_shapes=scratch,
        compiler_params=pltpu.CompilerParams(
            collective_id=0, has_side_effects=True, vmem_limit_bytes=50000000
        ),
    )(*(pltpu.with_memory_space_constraint(v, pltpu.HBM) for v in (rows_of(raw_states), rows_of(phases), rows_of(levels), window)))
    return both[:4].reshape(1, 2, 2, LANES) * (1.0 / 256.0), both[4, :1]


def solution(mesh):
    in_specs = (
        P(None, "st", None, "lat", None),
        P(None, "lat", None),
        P(None, "lat", None),
        P("st"),
    )
    out_specs = (P(("lat", "st"), None, None, None), P(("lat", "st")))
    return jax.shard_map(local, mesh=mesh, in_specs=in_specs, out_specs=out_specs, check_vma=False)
```

```python
import functools
import itertools
import math

import jax
import jax.numpy as jnp
from jax import lax
from jax.experimental import pallas as pl
from jax.experimental.pallas import tpu as pltpu
from jax.sharding import PartitionSpec as P

ORDER = 6
WINDOWS = 16
LEVELS = 8
PHASES = 8
F32 = jnp.float32
BF16 = jnp.bfloat16
MESH = pl.DeviceIdType.MESH

hop_far = 0.25
level_step = 0.3
stagger = 0.4
spectrum = 6.0
broaden = 0.2
angle_low = 0.5
angle_high = 2.6
half_root = 0.5 * math.sqrt(3.0)

unit = 2.0 / spectrum
LAT = 16
ST = 8
NDEV = LAT * ST
BATCH = 32
LANES = 128
KX = 4
NH = 8

ON_A, ON_B, C0, S0, C1, S1, C2X, S2X, C1Y, S1Y, C2Y, S2Y = range(12)


def y_up(v):
    return pltpu.roll(v, v.shape[1] - 1, 1)


def y_down(v):
    return pltpu.roll(v, 1, 1)


def x_up(get, k):
    return get(k + 1) if k < KX - 1 else pltpu.roll(get(0), 7, 0)


def x_down(get, k):
    return get(k - 1) if k > 0 else pltpu.roll(get(KX - 1), 1, 0)


def mul(cr, ci, ur, ui):
    return cr * ur - ci * ui, cr * ui + ci * ur


def mulc(cr, ci, ur, ui):
    return cr * ur + ci * ui, cr * ui - ci * ur


def eighth_cos(q):
    e = 2.0 - jnp.minimum(q, 8.0 - q)
    r = math.sqrt(0.5)
    cubic = (1.0 - 2.0 * r) / 6.0
    return e * ((r - cubic) + cubic * (e * e))


def build_coefs(numbers, co, c2):
    planes = [jnp.transpose(numbers[:, t].astype(F32), (1, 0, 2)) for t in range(5)]
    for k in range(KX):
        kk, e = k // 2, k % 2

        def plane(t):
            return jnp.concatenate([planes[t][2 * h + e, kk * 8 : kk * 8 + 8] for h in range(NH)], axis=1)

        for t, (cp, sp) in enumerate(((C0, S0), (C1, S1), (0, 1))):
            q = plane(t)
            cosq = -unit * eighth_cos(q)
            qs = q + 6.0
            qs = jnp.where(qs >= 8.0, qs - 8.0, qs)
            sinq = -unit * eighth_cos(qs)
            if t < 2:
                co[cp, k] = cosq
                co[sp, k] = sinq
            else:
                c2[0, k] = cosq
                c2[1, k] = sinq
            if t == 1:
                co[C1Y, k] = y_up(cosq)
                co[S1Y, k] = y_up(sinq)
            if t == 2:
                co[C2Y, k] = y_up(cosq)
                co[S2Y, k] = y_up(sinq)
        for t, dst, par in ((3, ON_A, 1.0), (4, ON_B, -1.0)):
            co[dst, k] = unit * (level_step * (plane(t) - 0.5 * (LEVELS - 1)) + stagger * par)
    for k in range(KX):
        co[C2X, k] = x_down(lambda kk: c2[0, kk], k)
        co[S2X, k] = x_down(lambda kk: c2[1, kk], k)


def apply_h(get, co, k):
    beta = unit * hop_far
    u = [[get(c, s, k) for c in range(2)] for s in range(2)]
    up = [[x_up(functools.partial(get, c, s), k) for c in range(2)] for s in range(2)]
    dn = [[x_down(functools.partial(get, c, s), k) for c in range(2)] for s in range(2)]
    a = [[beta * (up[s][c] - u[s][c]) for c in range(2)] for s in range(2)]
    b = [[beta * (u[s][c] - dn[s][c]) for c in range(2)] for s in range(2)]
    near = mul(co[C0, k], co[S0, k], *u[1])
    r1 = mul(co[C1Y, k], co[S1Y, k], *u[1])
    r2 = mul(co[C2Y, k], co[S2Y, k], *up[1])
    on = co[ON_A, k]
    a_re = on * u[0][0] + near[0] - (a[0][1] + b[0][1]) + y_up(b[0][1]) + y_down(r1[0] + r2[0] + a[0][1])
    a_im = on * u[0][1] + near[1] + (a[0][0] + b[0][0]) - y_up(b[0][0]) + y_down(r1[1] + r2[1] - a[0][0])
    near = mulc(co[C0, k], co[S0, k], *u[0])
    q1 = mulc(co[C1, k], co[S1, k], *u[0])
    q2 = mulc(co[C2X, k], co[S2X, k], *dn[0])
    on = co[ON_B, k]
    b_re = on * u[1][0] + near[0] + (a[1][1] + b[1][1]) + y_up(q1[0] + q2[0] - b[1][1]) - y_down(a[1][1])
    b_im = on * u[1][1] + near[1] - (a[1][0] + b[1][0]) + y_up(q1[1] + q2[1] + b[1][0]) + y_down(a[1][0])
    return [[a_re, a_im], [b_re, b_im]]


def site_speeds(u, yu, du, xu, xd, yxd, dxu, w):
    inv = 1.0 / unit
    hf = hop_far * half_root
    vf = hop_far * 1.5
    pick = lambda v, s: (v[0][s], v[1][s])
    out = [[None, None], [None, None]]
    for s, sign in ((0, 1.0), (1, -1.0)):
        other = 1 - s
        if s == 0:
            n0 = mul(w[0], w[1], *pick(u, other))
            one = mul(w[2], w[3], *pick(du, other))
            two = mul(w[4], w[5], *pick(dxu, other))
        else:
            n0 = mulc(w[0], w[1], *pick(u, other))
            one = mulc(w[6], w[7], *pick(yu, other))
            two = mulc(w[8], w[9], *pick(yxd, other))
        dif = [(sign * inv * half_root) * (one[c] - two[c]) for c in range(2)]
        tot = [(sign * inv) * (0.5 * (one[c] + two[c]) - n0[c]) for c in range(2)]
        far_x = [(yu[c][s] + yxd[c][s]) + (du[c][s] + dxu[c][s]) - 2.0 * (xu[c][s] + xd[c][s]) for c in range(2)]
        far_y = [(yu[c][s] - yxd[c][s]) + (du[c][s] - dxu[c][s]) for c in range(2)]
        out[0][s] = [dif[1] + (sign * hf) * far_x[0], (sign * hf) * far_x[1] - dif[0]]
        out[1][s] = [tot[1] + (sign * vf) * far_y[0], (sign * vf) * far_y[1] - tot[0]]
    return out


def hops(dyl, dz, dx, dyh):
    return (1 if dyl else 2 * dyh) + min(dz, 4 - dz) + min(dx, 4 - dx)


OFFSETS = sorted(itertools.product(range(2), range(4), range(4), range(2)), key=lambda d: (-hops(*d), d))


def columns_of_chips(lat):
    yl, z = lat // 8, lax.rem(lat // 2, 4)
    offsets = [(1, 2), (0, 2), (1, 1), (1, 3), (0, 1), (0, 3), (1, 0)]
    return [lax.rem(yl + a, 2) * 8 + lax.rem(z + b, 4) * 2 for a, b in offsets]


LAT_ORDER = [(1, 2), (0, 2), (1, 1), (1, 3), (0, 1), (0, 3), (1, 0), (0, 0)]
ST_ORDER = [(2, 1), (1, 1), (3, 1), (2, 0), (0, 1), (1, 0), (3, 0), (0, 0)]


def coordinates(lat, st):
    yl, z, x, yh = lat // 8, lax.rem(lat // 2, 4), st // 2, lax.rem(st, 2)
    rows = {(a, b): lax.rem(yl + a, 2) * 8 + lax.rem(z + b, 4) * 2 for a, b in LAT_ORDER}
    columns = {(a, b): lax.rem(x + a, 4) * 2 + lax.rem(yh + b, 2) for a, b in ST_ORDER}
    return rows, columns


def chips(lat, st):
    rows, columns = coordinates(lat, st)
    return [(rows[d[:2]], columns[d[2:]]) for d in OFFSETS if any(d)]


def kernel(
    raw, phases, levels, window, both,
    win_s, ph_v, lev_v, c_send, c_recv, r_recv, co, c2, field, total, low,
    row_w, tmp_w, m_send, m_recv, left, right, part, s_recv, e_send, e_recv, f_send, f_recv,
    in_sem, r_sem, c_sem, c_in, d_sem, m_out, m_in, s_sem, e_sem, f_sem, known,
):
    lat = lax.axis_index("lat")
    st = lax.axis_index("st")
    state = st * LAT + lat
    me = lat * ST + st
    slot = lax.rem(lat, 2) * 8 + lat // 2
    core = lax.rem(lat, 2)
    twin = lat + 1 - 2 * core

    def remote(src, dst, out_sem, in_sem, row, column):
        return pltpu.make_async_remote_copy(
            src, dst, out_sem, in_sem, device_id=(row, column), device_id_type=MESH
        )

    def wait_for(ref, sem):
        pltpu.make_async_copy(ref, ref, sem).wait()

    load_ph = pltpu.make_async_copy(phases, ph_v, in_sem.at[0])
    load_lev = pltpu.make_async_copy(levels, lev_v, in_sem.at[1])
    load_win = pltpu.make_async_copy(window, win_s, in_sem.at[2])
    load_ph.start()
    load_lev.start()
    load_win.start()
    near = columns_of_chips(lat)
    x, yh = st // 2, lax.rem(st, 2)
    along = [lax.rem(x + i, 4) * 2 + yh for i in (1, 3)]
    across = (lax.rem(lat + 8, LAT), st + 1 - 2 * yh)

    def greet(sem, row, column):
        pl.semaphore_signal(sem, inc=1, device_id=(row, column), device_id_type=MESH)

    barrier = pltpu.get_barrier_semaphore()
    for row in near:
        greet(barrier, row, st)
        greet(barrier, row + 1, st)
    for column in along:
        greet(barrier, lat, column)
    greet(barrier, *across)
    greet(barrier, twin, st)
    load_ph.wait()
    load_lev.wait()
    load_win.wait()
    c_send[0:3] = ph_v[...].astype(F32).astype(BF16)
    c_send[3:5] = lev_v[...].astype(F32).astype(BF16)
    pl.semaphore_wait(barrier, LAT - 1 + 3)

    mine = lat // 2
    for row in near:
        remote(c_send, c_recv.at[slot], c_sem.at[0], c_in.at[mine], row + core, st).start()
    remote(c_send, c_recv.at[slot], d_sem.at[0], d_sem.at[1], twin, st).start()
    pltpu.make_async_copy(c_send, c_recv.at[slot], c_sem.at[1]).start()
    for row in near:
        for c in range(2):
            remote(raw.at[:, row + c], r_recv.at[slot], r_sem.at[0], r_sem.at[1], row + c, st).start()
    remote(raw.at[:, twin], r_recv.at[slot], r_sem.at[0], r_sem.at[1], twin, st).start()
    pltpu.make_async_copy(raw.at[:, lat], r_recv.at[slot], r_sem.at[1]).start()
    for row in near:
        greet(known.at[0], row, st)
        greet(known.at[0], row + 1, st)
    greet(known.at[0], twin, st)

    w = angle_low + (angle_high - angle_low) * jnp.full((8, LANES), win_s[lat], jnp.int32).astype(F32) / (
        WINDOWS - 1
    )
    cosines = [jnp.ones((8, LANES), F32), jnp.cos(w)]
    for _ in range(2, ORDER + 1):
        cosines.append(2.0 * cosines[1] * cosines[-1] - cosines[-2])

    for row in reversed(near):
        row = row + core
        held = c_recv.at[core * 8 + row // 2]
        wait_for(held, c_in.at[row // 2])
        remote(held, held, d_sem.at[0], d_sem.at[1], twin, st).start()
    pl.semaphore_wait(known.at[0], LAT - 1)
    for column in along:
        greet(known.at[1], lat, column)
    wait_for(c_recv.at[slot], c_sem.at[1])
    wait_for(c_recv.at[pl.ds(0, LAT // 2)], d_sem.at[1])

    build_coefs(c_recv, co, c2)

    pl.semaphore_wait(known.at[1], 2)
    for column in along:
        greet(known.at[2], lat, column)
    wait_for(r_recv, r_sem.at[1])

    def wide(v):
        return jnp.concatenate([v] * NH, axis=1)

    coef = [wide(cosines[0])] + [wide(2.0 * v) for v in cosines[1:]]
    for c in range(2):
        for s in range(2):
            block = jnp.transpose(r_recv[:, c, s].astype(F32), (1, 0, 2))
            for k in range(KX):
                kk, e = k // 2, k % 2
                field[0, c, s, k] = jnp.concatenate(
                    [block[2 * h + e, kk * 8 : kk * 8 + 8] for h in range(NH)], axis=1
                )

    for degree in range(1, ORDER + 1):
        now, new = (degree - 1) % 2, degree % 2
        get = lambda c, s, k: field[now, c, s, k]
        for k in range(KX):
            out = apply_h(get, co, k)
            for s in range(2):
                for c in range(2):
                    if degree == 1:
                        v = 0.5 * out[s][c]
                        total[c, s, k] = field[0, c, s, k] + coef[1] * v
                    else:
                        v = out[s][c] - field[new, c, s, k]
                        psi = total[c, s, k] + coef[degree] * v
                        total[c, s, k] = psi
                        if degree == ORDER:
                            low[c, s, k] = psi.astype(BF16).astype(F32)
                    if degree < ORDER:
                        field[new, c, s, k] = v

    pl.semaphore_wait(known.at[2], 2)
    far = chips(lat, st)
    rows, columns = coordinates(lat, st)
    lane8 = lax.broadcasted_iota(jnp.int32, (8, LANES), 1)
    low8 = lane8 < 64
    half8 = lax.rem(lane8, 64)

    packed = [[None] * 12 for _ in range(2 * NH)]
    for c in range(2):
        for s in range(2):
            get = functools.partial(lambda c, s, k: low[c, s, k], c, s)
            column = {k: get(k) for k in range(KX)}
            column[-1] = x_down(get, 0)
            column[KX] = x_up(get, KX - 1)
            for i in range(3):
                for h in range(NH):
                    one = column[i - 1][:, h * LANES : (h + 1) * LANES]
                    two = column[i + 2][:, h * LANES : (h + 1) * LANES]
                    r = (c * 2 + s) * 3 + i
                    packed[2 * h][r] = jnp.where(low8, one, pltpu.roll(two, 64, 1))
                    packed[2 * h + 1][r] = jnp.where(low8, pltpu.roll(one, 64, 1), two)
    for j in range(2 * NH):
        after, before = packed[(j + 1) % 16], packed[j - 1]
        ends = jnp.zeros((8, LANES), F32)
        for r in range(12):
            up = pltpu.roll(after[r], 63 - r, 1)
            down = pltpu.roll(before[r], 65 + r, 1)
            ends = jnp.where(half8 == 63 - r, up, jnp.where(half8 == r, down, ends))
        rows16 = jnp.stack(packed[j] + [ends] * 4, axis=0)
        m_send[:, j % 2, j // 2] = jnp.transpose(rows16, (1, 0, 2)).astype(BF16)

    for q in ST_ORDER:
        column = columns[q]
        for a in LAT_ORDER:
            for c in range(2):
                if any(q) or any(a):
                    p = rows[a] + c
                    remote(m_send.at[p // 2, c, column], m_recv.at[state], m_out, m_in.at[st], p, column).start()
    remote(m_send.at[mine, 1 - core, st], m_recv.at[state], m_out, m_in.at[st], twin, st).start()
    pltpu.make_async_copy(m_send.at[mine, core, st], m_recv.at[state], m_in.at[st]).start()

    numer = jnp.zeros((8, NH * LANES), F32)
    denom = jnp.zeros((8, NH * LANES), F32)
    get = lambda c, s, k: total[c, s, k]
    for k in range(KX):
        out = apply_h(get, co, k)
        for s in range(2):
            for c in range(2):
                v = total[c, s, k]
                numer = numer + v * out[s][c]
                denom = denom + v * v
    energy = jnp.sum(numer) / jnp.sum(denom) * (1.0 / unit)
    lane = lax.broadcasted_iota(jnp.int32, (1, LANES), 1)
    e_send[...] = jnp.where(lane == state, jnp.full((1, LANES), energy, F32), 0.0)
    for i in range(1, LAT):
        remote(e_send, e_recv.at[lat], e_sem.at[0], e_sem.at[1], lax.rem(lat + i, LAT), st).start()
    pltpu.make_async_copy(e_send, e_recv.at[lat], e_sem.at[1]).start()

    line = lat // 2
    chunk = pl.ds(pl.multiple_of(st * LANES, LANES), LANES)
    low1 = lane < 64
    for j, plane in enumerate((C2X, S2X)):
        for k in range(KX):
            tmp_w[j, k] = y_up(co[plane, k])

    this_line = lax.broadcasted_iota(jnp.int32, (8, LANES), 0) == line

    def weight_row(j, k):
        if j in (4, 5):
            v = c2[j - 4, k, :, chunk]
        elif j in (8, 9):
            v = tmp_w[j - 8, k, :, chunk]
        else:
            v = co[(C0, S0, C1, S1, None, None, C1Y, S1Y)[j], k, :, chunk]
        return jnp.sum(jnp.where(this_line, v, 0.0), axis=0, keepdims=True)

    for j in range(10):
        rows = [weight_row(j, k) for k in range(KX)]
        swapped = [pltpu.roll(v, 64, 1) for v in rows]
        for t, (k1, k2) in enumerate(((0, 3), (1, 2))):
            first_half = jnp.where(low1, rows[k1], swapped[k2])
            second_half = jnp.where(low1, swapped[k1], rows[k2])
            row_w[2 * j + t : 2 * j + t + 1, :] = jnp.where(core == 0, first_half, second_half)

    lane16 = lax.broadcasted_iota(jnp.int32, (BATCH, LANES), 1)
    low16 = lane16 < 64
    top16 = lax.rem(lane16, 64) == 63
    bottom16 = lax.rem(lane16, 64) == 0

    def turn(v, by):
        return v if by % LANES == 0 else pltpu.roll(v, by % LANES, 1)

    def halves(one, two):
        return jnp.where(low16, one, two)

    @pl.loop(0, NDEV // BATCH)
    def _(i):
        firsts = []
        for at_once in range(BATCH // LAT):
            dx, dyh = jnp.int32(0), jnp.int32(0)
            for j, (one, two) in enumerate(ST_ORDER):
                if j % (BATCH // LAT) == at_once:
                    dx = jnp.where(i == j // (BATCH // LAT), one, dx)
                    dyh = jnp.where(i == j // (BATCH // LAT), two, dyh)
            group = lax.rem(x + 4 - dx, 4) * 2 + lax.rem(yh + dyh, 2)
            first = pl.multiple_of(group * LAT, LAT)
            firsts.append(first)
            wait_for(m_recv.at[pl.ds(first, LAT)], m_in.at[group])
        by_row = [
            jnp.transpose(m_recv[pl.ds(first, LAT)].astype(F32), (1, 0, 2)) for first in firsts
        ]
        block = by_row[0] if len(by_row) == 1 else jnp.concatenate(by_row, axis=1)

        def put(ref, lead, j, v):
            v = v.astype(BF16)
            for at_once, first in enumerate(firsts):
                ref[lead, pl.ds(first, LAT), j * LANES : (j + 1) * LANES] = v[at_once * LAT : (at_once + 1) * LAT]

        ends = block[12]
        us, yus, dus, xus, xds, yxds, dxus = [[[[None, None], [None, None]] for _ in range(2)] for _ in range(7)]
        for c in range(2):
            for s in range(2):
                v, up, down = [], [], []
                for k in range(3):
                    r = (c * 2 + s) * 3 + k
                    row = block[r]
                    v.append(row)
                    up.append(jnp.where(top16, turn(ends, r), turn(row, -1)))
                    down.append(jnp.where(bottom16, turn(ends, -r), turn(row, 1)))
                us[0][c][s], xus[0][c][s], xds[0][c][s] = v[1], v[2], v[0]
                yus[0][c][s], yxds[0][c][s] = up[1], up[0]
                dus[0][c][s], dxus[0][c][s] = down[1], down[2]
                us[1][c][s] = halves(v[2], v[0])
                xus[1][c][s] = halves(turn(v[0], 64), v[1])
                xds[1][c][s] = halves(v[1], turn(v[2], 64))
                yus[1][c][s] = halves(up[2], up[0])
                yxds[1][c][s] = halves(up[1], turn(up[2], 64))
                dus[1][c][s] = halves(down[2], down[0])
                dxus[1][c][s] = halves(turn(down[0], 64), down[1])
        for t in range(2):
            w = [jnp.broadcast_to(row_w[2 * j + t : 2 * j + t + 1, :], (BATCH, LANES)) for j in range(10)]
            out = site_speeds(us[t], yus[t], dus[t], xus[t], xds[t], yxds[t], dxus[t], w)
            for c in range(2):
                for s in range(2):
                    j = c * 4 + s * 2 + t
                    js = (j + 4) % 8
                    v = us[t][c][s]
                    put(right, 0, j, v)
                    put(right, 1, js, v if j >= 4 else -v)
                    for a in range(2):
                        put(left, a, j, out[a][s][c])

    for a in range(2):
        for c in range(2):
            prod = lax.dot_general(left[a], right[c], (((1,), (1,)), ((), ())), preferred_element_type=F32)
            part[:, 2 * a + c, :] = prod

    for row, column in far:
        for c in range(2):
            p = row + c
            remote(part.at[p * ST + column], s_recv.at[me], s_sem.at[0], s_sem.at[1], p, column).start()
    remote(part.at[twin * ST + st], s_recv.at[me], s_sem.at[0], s_sem.at[1], twin, st).start()
    pltpu.make_async_copy(part.at[me], s_recv.at[me], s_sem.at[1]).start()

    wait_for(e_recv, e_sem.at[1])
    f_send[...] = jnp.sum(e_recv[...], axis=0)
    for i in range(1, ST):
        remote(f_send, f_recv.at[st], f_sem.at[0], f_sem.at[1], lat, lax.rem(st + i, ST)).start()
    pltpu.make_async_copy(f_send, f_recv.at[st], f_sem.at[1]).start()

    wait_for(f_recv, f_sem.at[1])
    energies = jnp.sum(f_recv[...], axis=0)
    own = jnp.sum(jnp.where(lane == me, energies, 0.0), axis=1, keepdims=True)
    differ = own - energies
    weight = differ / (differ * differ + broaden * broaden)

    wait_for(s_recv, s_sem.at[1])

    sums = jnp.sum(s_recv[...], axis=0)
    velocity = sums * (1.0 / 256.0)
    both[0:4] = sums
    cross = velocity[1:2] * velocity[2:3] - velocity[0:1] * velocity[3:4]
    both[4:5] = jnp.broadcast_to(jnp.sum(weight * cross, axis=1, keepdims=True), (1, LANES))

    wait_for(c_recv.at[pl.ds(0, LAT // 2 - 1)], c_sem.at[0])
    wait_for(c_recv.at[pl.ds(0, LAT // 2)], d_sem.at[0])
    wait_for(r_recv.at[pl.ds(0, LAT - 1)], r_sem.at[0])
    wait_for(e_recv.at[pl.ds(0, LAT - 1)], e_sem.at[0])
    wait_for(f_recv.at[pl.ds(0, ST - 1)], f_sem.at[0])
    wait_for(m_recv.at[pl.ds(0, NDEV - 1)], m_out)
    wait_for(s_recv.at[pl.ds(0, NDEV - 1)], s_sem.at[0])


def rows_of(array):
    head = array.shape[:-2]
    array = array.reshape(head + (2, NH, LANES))
    return jnp.swapaxes(array, -3, -2).reshape(head + (2 * NH, LANES))


def local(raw_states, levels, phases, window):
    vm = pltpu.VMEM
    dma = pltpu.SemaphoreType.DMA
    scratch = [
        pltpu.SMEM((LAT,), jnp.int32),
        vm((3, 16, LANES), jnp.int32), vm((2, 16, LANES), jnp.int32),
        vm((5, 16, LANES), BF16), vm((LAT, 5, 16, LANES), BF16),
        vm((LAT, 2, 2, 16, LANES), BF16),
        vm((12, KX, 8, NH * LANES), F32), vm((2, KX, 8, NH * LANES), F32),
        vm((2, 2, 2, KX, 8, NH * LANES), F32), vm((2, 2, KX, 8, NH * LANES), F32),
        vm((2, 2, KX, 8, NH * LANES), F32),
        vm((24, LANES), F32), vm((2, KX, 8, NH * LANES), F32),
        vm((8, 2, ST, 16, LANES), BF16), vm((NDEV, 16, LANES), BF16),
        vm((2, NDEV, 1024), BF16), vm((2, NDEV, 1024), BF16),
        vm((NDEV, 4, LANES), F32), vm((NDEV, 4, LANES), F32),
        vm((1, LANES), F32), vm((LAT, 1, LANES), F32),
        vm((1, LANES), F32), vm((ST, 1, LANES), F32),
        dma((3,)), dma((2,)), dma((2,)), dma((LAT // 2,)), dma((2,)), dma, dma((ST,)), dma((2,)), dma((2,)), dma((2,)),
        pltpu.SemaphoreType.REGULAR((3,)),
    ]
    hbm = pl.BlockSpec(memory_space=pltpu.HBM)
    both = pl.pallas_call(
        kernel,
        out_shape=jax.ShapeDtypeStruct((8, LANES), F32),
        in_specs=[hbm] * 4,
        out_specs=pl.BlockSpec(memory_space=pltpu.VMEM),
        scratch_shapes=scratch,
        compiler_params=pltpu.CompilerParams(
            collective_id=0, has_side_effects=True, vmem_limit_bytes=50000000
        ),
    )(*(pltpu.with_memory_space_constraint(v, pltpu.HBM) for v in (rows_of(raw_states), rows_of(phases), rows_of(levels), window)))
    return both[:4].reshape(1, 2, 2, LANES) * (1.0 / 256.0), both[4, :1]


def solution(mesh):
    in_specs = (
        P(None, "st", None, "lat", None),
        P(None, "lat", None),
        P(None, "lat", None),
        P("st"),
    )
    out_specs = (P(("lat", "st"), None, None, None), P(("lat", "st")))
    return jax.shard_map(local, mesh=mesh, in_specs=in_specs, out_specs=out_specs, check_vma=False)
```

```python
import functools
import itertools
import math

import jax
import jax.numpy as jnp
from jax import lax
from jax.experimental import pallas as pl
from jax.experimental.pallas import tpu as pltpu
from jax.sharding import PartitionSpec as P

ORDER = 6
WINDOWS = 16
LEVELS = 8
PHASES = 8
F32 = jnp.float32
BF16 = jnp.bfloat16
MESH = pl.DeviceIdType.MESH

hop_far = 0.25
level_step = 0.3
stagger = 0.4
spectrum = 6.0
broaden = 0.2
angle_low = 0.5
angle_high = 2.6
half_root = 0.5 * math.sqrt(3.0)

unit = 2.0 / spectrum
LAT = 16
ST = 8
NDEV = LAT * ST
BATCH = 32
LANES = 128
KX = 4
NH = 8

ON_A, ON_B, C0, S0, C1, S1, C2X, S2X, C1Y, S1Y, C2Y, S2Y = range(12)


def y_up(v):
    return pltpu.roll(v, v.shape[1] - 1, 1)


def y_down(v):
    return pltpu.roll(v, 1, 1)


def x_up(get, k):
    return get(k + 1) if k < KX - 1 else pltpu.roll(get(0), 7, 0)


def x_down(get, k):
    return get(k - 1) if k > 0 else pltpu.roll(get(KX - 1), 1, 0)


def mul(cr, ci, ur, ui):
    return cr * ur - ci * ui, cr * ui + ci * ur


def mulc(cr, ci, ur, ui):
    return cr * ur + ci * ui, cr * ui - ci * ur


def eighth_cos(q):
    e = 2.0 - jnp.minimum(q, 8.0 - q)
    r = math.sqrt(0.5)
    cubic = (1.0 - 2.0 * r) / 6.0
    return e * ((r - cubic) + cubic * (e * e))


def build_coefs(numbers, co, c2):
    planes = [jnp.transpose(numbers[:, t].astype(F32), (1, 0, 2)) for t in range(5)]
    for k in range(KX):
        kk, e = k // 2, k % 2

        def plane(t):
            return jnp.concatenate([planes[t][2 * h + e, kk * 8 : kk * 8 + 8] for h in range(NH)], axis=1)

        for t, (cp, sp) in enumerate(((C0, S0), (C1, S1), (0, 1))):
            q = plane(t)
            cosq = (-1.0 / hop_far) * eighth_cos(q)
            qs = q + 6.0
            qs = jnp.where(qs >= 8.0, qs - 8.0, qs)
            sinq = (-1.0 / hop_far) * eighth_cos(qs)
            if t < 2:
                co[cp, k] = cosq
                co[sp, k] = sinq
            else:
                c2[0, k] = cosq
                c2[1, k] = sinq
            if t == 1:
                co[C1Y, k] = y_up(cosq)
                co[S1Y, k] = y_up(sinq)
            if t == 2:
                co[C2Y, k] = y_up(cosq)
                co[S2Y, k] = y_up(sinq)
        for t, dst, par in ((3, ON_A, 1.0), (4, ON_B, -1.0)):
            co[dst, k] = (1.0 / hop_far) * (level_step * (plane(t) - 0.5 * (LEVELS - 1)) + stagger * par)
    for k in range(KX):
        co[C2X, k] = x_down(lambda kk: c2[0, kk], k)
        co[S2X, k] = x_down(lambda kk: c2[1, kk], k)


def apply_h(get, co, k, before=None):
    u = [[get(c, s, k) for c in range(2)] for s in range(2)]
    up = [[x_up(functools.partial(get, c, s), k) for c in range(2)] for s in range(2)]
    dn = [[x_down(functools.partial(get, c, s), k) for c in range(2)] for s in range(2)]
    a = [[up[s][c] - u[s][c] for c in range(2)] for s in range(2)]
    b = before if before else [[u[s][c] - dn[s][c] for c in range(2)] for s in range(2)]
    near = mul(co[C0, k], co[S0, k], *u[1])
    r1 = mul(co[C1Y, k], co[S1Y, k], *u[1])
    r2 = mul(co[C2Y, k], co[S2Y, k], *up[1])
    on = co[ON_A, k]
    a_re = on * u[0][0] + near[0] - (a[0][1] + b[0][1]) + y_up(b[0][1]) + y_down(r1[0] + r2[0] + a[0][1])
    a_im = on * u[0][1] + near[1] + (a[0][0] + b[0][0]) - y_up(b[0][0]) + y_down(r1[1] + r2[1] - a[0][0])
    near = mulc(co[C0, k], co[S0, k], *u[0])
    q1 = mulc(co[C1, k], co[S1, k], *u[0])
    q2 = mulc(co[C2X, k], co[S2X, k], *dn[0])
    on = co[ON_B, k]
    b_re = on * u[1][0] + near[0] + (a[1][1] + b[1][1]) + y_up(q1[0] + q2[0] - b[1][1]) - y_down(a[1][1])
    b_im = on * u[1][1] + near[1] - (a[1][0] + b[1][0]) + y_up(q1[1] + q2[1] + b[1][0]) + y_down(a[1][0])
    return [[a_re, a_im], [b_re, b_im]], a


def site_speeds(u, yu, du, xu, xd, yxd, dxu, w):
    inv = hop_far
    hf = hop_far * half_root
    vf = hop_far * 1.5
    pick = lambda v, s: (v[0][s], v[1][s])
    out = [[None, None], [None, None]]
    for s, sign in ((0, 1.0), (1, -1.0)):
        other = 1 - s
        if s == 0:
            n0 = mul(w[0], w[1], *pick(u, other))
            one = mul(w[2], w[3], *pick(du, other))
            two = mul(w[4], w[5], *pick(dxu, other))
        else:
            n0 = mulc(w[0], w[1], *pick(u, other))
            one = mulc(w[6], w[7], *pick(yu, other))
            two = mulc(w[8], w[9], *pick(yxd, other))
        dif = [(sign * inv * half_root) * (one[c] - two[c]) for c in range(2)]
        tot = [(sign * inv) * (0.5 * (one[c] + two[c]) - n0[c]) for c in range(2)]
        far_x = [(yu[c][s] + yxd[c][s]) + (du[c][s] + dxu[c][s]) - 2.0 * (xu[c][s] + xd[c][s]) for c in range(2)]
        far_y = [(yu[c][s] - yxd[c][s]) + (du[c][s] - dxu[c][s]) for c in range(2)]
        out[0][s] = [dif[1] + (sign * hf) * far_x[0], (sign * hf) * far_x[1] - dif[0]]
        out[1][s] = [tot[1] + (sign * vf) * far_y[0], (sign * vf) * far_y[1] - tot[0]]
    return out


def hops(dyl, dz, dx, dyh):
    return (1 if dyl else 2 * dyh) + min(dz, 4 - dz) + min(dx, 4 - dx)


OFFSETS = sorted(itertools.product(range(2), range(4), range(4), range(2)), key=lambda d: (-hops(*d), d))


def columns_of_chips(lat):
    yl, z = lat // 8, lax.rem(lat // 2, 4)
    offsets = [(1, 2), (0, 2), (1, 1), (1, 3), (0, 1), (0, 3), (1, 0)]
    return [lax.rem(yl + a, 2) * 8 + lax.rem(z + b, 4) * 2 for a, b in offsets]


LAT_ORDER = [(1, 2), (0, 2), (1, 1), (1, 3), (0, 1), (0, 3), (1, 0), (0, 0)]
ST_ORDER = [(2, 1), (1, 1), (3, 1), (2, 0), (0, 1), (1, 0), (3, 0), (0, 0)]


def coordinates(lat, st):
    yl, z, x, yh = lat // 8, lax.rem(lat // 2, 4), st // 2, lax.rem(st, 2)
    rows = {(a, b): lax.rem(yl + a, 2) * 8 + lax.rem(z + b, 4) * 2 for a, b in LAT_ORDER}
    columns = {(a, b): lax.rem(x + a, 4) * 2 + lax.rem(yh + b, 2) for a, b in ST_ORDER}
    return rows, columns


def chips(lat, st):
    rows, columns = coordinates(lat, st)
    return [(rows[d[:2]], columns[d[2:]]) for d in OFFSETS if any(d)]


def kernel(
    raw, phases, levels, window, both,
    win_s, ph_v, lev_v, c_send, c_recv, r_recv, co, c2, field, total, low,
    row_w, tmp_w, m_send, m_recv, left, right, part, s_recv, e_send, e_recv, f_send, f_recv,
    in_sem, r_sem, c_sem, c_in, d_sem, m_out, m_in, s_sem, e_sem, f_sem, known,
):
    lat = lax.axis_index("lat")
    st = lax.axis_index("st")
    state = st * LAT + lat
    me = lat * ST + st
    slot = lax.rem(lat, 2) * 8 + lat // 2
    core = lax.rem(lat, 2)
    twin = lat + 1 - 2 * core

    def remote(src, dst, out_sem, in_sem, row, column):
        return pltpu.make_async_remote_copy(
            src, dst, out_sem, in_sem, device_id=(row, column), device_id_type=MESH
        )

    def wait_for(ref, sem):
        pltpu.make_async_copy(ref, ref, sem).wait()

    load_ph = pltpu.make_async_copy(phases, ph_v, in_sem.at[0])
    load_lev = pltpu.make_async_copy(levels, lev_v, in_sem.at[1])
    load_win = pltpu.make_async_copy(window, win_s, in_sem.at[2])
    load_ph.start()
    load_lev.start()
    load_win.start()
    near = columns_of_chips(lat)
    x, yh = st // 2, lax.rem(st, 2)
    along = [lax.rem(x + i, 4) * 2 + yh for i in (1, 3)]
    across = (lax.rem(lat + 8, LAT), st + 1 - 2 * yh)

    def greet(sem, row, column):
        pl.semaphore_signal(sem, inc=1, device_id=(row, column), device_id_type=MESH)

    barrier = pltpu.get_barrier_semaphore()
    for row in near:
        greet(barrier, row, st)
        greet(barrier, row + 1, st)
    for column in along:
        greet(barrier, lat, column)
    greet(barrier, *across)
    greet(barrier, twin, st)
    load_ph.wait()
    load_lev.wait()
    load_win.wait()
    c_send[0:3] = ph_v[...].astype(F32).astype(BF16)
    c_send[3:5] = lev_v[...].astype(F32).astype(BF16)
    pl.semaphore_wait(barrier, LAT - 1 + 3)

    mine = lat // 2
    for row in near:
        remote(c_send, c_recv.at[slot], c_sem.at[0], c_in.at[mine], row + core, st).start()
    remote(c_send, c_recv.at[slot], d_sem.at[0], d_sem.at[1], twin, st).start()
    pltpu.make_async_copy(c_send, c_recv.at[slot], c_sem.at[1]).start()
    for row in near:
        for c in range(2):
            remote(raw.at[:, row + c], r_recv.at[slot], r_sem.at[0], r_sem.at[1], row + c, st).start()
    remote(raw.at[:, twin], r_recv.at[slot], r_sem.at[0], r_sem.at[1], twin, st).start()
    pltpu.make_async_copy(raw.at[:, lat], r_recv.at[slot], r_sem.at[1]).start()
    for row in near:
        greet(known.at[0], row, st)
        greet(known.at[0], row + 1, st)
    greet(known.at[0], twin, st)

    w = angle_low + (angle_high - angle_low) * jnp.full((8, LANES), win_s[lat], jnp.int32).astype(F32) / (
        WINDOWS - 1
    )
    cosines = [jnp.ones((8, LANES), F32), jnp.cos(w)]
    for _ in range(2, ORDER + 1):
        cosines.append(2.0 * cosines[1] * cosines[-1] - cosines[-2])

    for row in reversed(near):
        row = row + core
        held = c_recv.at[core * 8 + row // 2]
        wait_for(held, c_in.at[row // 2])
        remote(held, held, d_sem.at[0], d_sem.at[1], twin, st).start()
    pl.semaphore_wait(known.at[0], LAT - 1)
    for column in along:
        greet(known.at[1], lat, column)
    wait_for(c_recv.at[slot], c_sem.at[1])
    wait_for(c_recv.at[pl.ds(0, LAT // 2)], d_sem.at[1])

    build_coefs(c_recv, co, c2)

    pl.semaphore_wait(known.at[1], 2)
    for column in along:
        greet(known.at[2], lat, column)
    wait_for(r_recv, r_sem.at[1])

    def wide(v):
        return jnp.concatenate([v] * NH, axis=1)

    coef = [wide(cosines[0])] + [wide(2.0 * v) for v in cosines[1:]]
    for c in range(2):
        for s in range(2):
            block = jnp.transpose(r_recv[:, c, s].astype(F32), (1, 0, 2))
            for k in range(KX):
                kk, e = k // 2, k % 2
                field[0, c, s, k] = jnp.concatenate(
                    [block[2 * h + e, kk * 8 : kk * 8 + 8] for h in range(NH)], axis=1
                )

    for degree in range(1, ORDER + 1):
        now, new = (degree - 1) % 2, degree % 2
        get = lambda c, s, k: field[now, c, s, k]
        step = None
        for k in range(KX):
            out, step = apply_h(get, co, k, step)
            for s in range(2):
                for c in range(2):
                    if degree == 1:
                        v = (0.5 * unit * hop_far) * out[s][c]
                        total[c, s, k] = field[0, c, s, k] + coef[1] * v
                    else:
                        v = (unit * hop_far) * out[s][c] - field[new, c, s, k]
                        psi = total[c, s, k] + coef[degree] * v
                        total[c, s, k] = psi
                        if degree == ORDER:
                            low[c, s, k] = psi.astype(BF16).astype(F32)
                    if degree < ORDER:
                        field[new, c, s, k] = v

    pl.semaphore_wait(known.at[2], 2)
    far = chips(lat, st)
    rows, columns = coordinates(lat, st)
    lane8 = lax.broadcasted_iota(jnp.int32, (8, LANES), 1)
    low8 = lane8 < 64
    half8 = lax.rem(lane8, 64)

    packed = [[None] * 12 for _ in range(2 * NH)]
    for c in range(2):
        for s in range(2):
            get = functools.partial(lambda c, s, k: low[c, s, k], c, s)
            column = {k: get(k) for k in range(KX)}
            column[-1] = x_down(get, 0)
            column[KX] = x_up(get, KX - 1)
            for i in range(3):
                for h in range(NH):
                    one = column[i - 1][:, h * LANES : (h + 1) * LANES]
                    two = column[i + 2][:, h * LANES : (h + 1) * LANES]
                    r = (c * 2 + s) * 3 + i
                    packed[2 * h][r] = jnp.where(low8, one, pltpu.roll(two, 64, 1))
                    packed[2 * h + 1][r] = jnp.where(low8, pltpu.roll(one, 64, 1), two)
    for j in range(2 * NH):
        after, before = packed[(j + 1) % 16], packed[j - 1]
        ends = jnp.zeros((8, LANES), F32)
        for r in range(12):
            up = pltpu.roll(after[r], 63 - r, 1)
            down = pltpu.roll(before[r], 65 + r, 1)
            ends = jnp.where(half8 == 63 - r, up, jnp.where(half8 == r, down, ends))
        rows16 = jnp.stack(packed[j] + [ends] * 4, axis=0)
        m_send[:, j % 2, j // 2] = jnp.transpose(rows16, (1, 0, 2)).astype(BF16)

    for row, column in far:
        for c in range(2):
            p = row + c
            remote(m_send.at[p // 2, c, column], m_recv.at[state], m_out, m_in.at[st], p, column).start()
    remote(m_send.at[mine, 1 - core, st], m_recv.at[state], m_out, m_in.at[st], twin, st).start()
    pltpu.make_async_copy(m_send.at[mine, core, st], m_recv.at[state], m_in.at[st]).start()

    numer = jnp.zeros((8, NH * LANES), F32)
    denom = jnp.zeros((8, NH * LANES), F32)
    get = lambda c, s, k: total[c, s, k]
    step = None
    for k in range(KX):
        out, step = apply_h(get, co, k, step)
        for s in range(2):
            for c in range(2):
                v = total[c, s, k]
                numer = numer + v * out[s][c]
                denom = denom + v * v
    energy = jnp.sum(numer) / jnp.sum(denom) * hop_far
    lane = lax.broadcasted_iota(jnp.int32, (1, LANES), 1)
    e_send[...] = jnp.where(lane == state, jnp.full((1, LANES), energy, F32), 0.0)
    for i in range(1, LAT):
        remote(e_send, e_recv.at[lat], e_sem.at[0], e_sem.at[1], lax.rem(lat + i, LAT), st).start()
    pltpu.make_async_copy(e_send, e_recv.at[lat], e_sem.at[1]).start()

    line = lat // 2
    chunk = pl.ds(pl.multiple_of(st * LANES, LANES), LANES)
    low1 = lane < 64
    for j, plane in enumerate((C2X, S2X)):
        for k in range(KX):
            tmp_w[j, k] = y_up(co[plane, k])

    this_line = lax.broadcasted_iota(jnp.int32, (8, LANES), 0) == line

    def weight_row(j, k):
        if j in (4, 5):
            v = c2[j - 4, k, :, chunk]
        elif j in (8, 9):
            v = tmp_w[j - 8, k, :, chunk]
        else:
            v = co[(C0, S0, C1, S1, None, None, C1Y, S1Y)[j], k, :, chunk]
        return jnp.sum(jnp.where(this_line, v, 0.0), axis=0, keepdims=True)

    for j in range(10):
        rows = [weight_row(j, k) for k in range(KX)]
        swapped = [pltpu.roll(v, 64, 1) for v in rows]
        for t, (k1, k2) in enumerate(((0, 3), (1, 2))):
            first_half = jnp.where(low1, rows[k1], swapped[k2])
            second_half = jnp.where(low1, swapped[k1], rows[k2])
            row_w[2 * j + t : 2 * j + t + 1, :] = jnp.where(core == 0, first_half, second_half)

    lane16 = lax.broadcasted_iota(jnp.int32, (BATCH, LANES), 1)
    low16 = lane16 < 64
    top16 = lax.rem(lane16, 64) == 63
    bottom16 = lax.rem(lane16, 64) == 0

    def turn(v, by):
        return v if by % LANES == 0 else pltpu.roll(v, by % LANES, 1)

    def halves(one, two):
        return jnp.where(low16, one, two)

    @pl.loop(0, NDEV // BATCH)
    def _(i):
        firsts = []
        for at_once in range(BATCH // LAT):
            turn_no = i * (BATCH // LAT) + at_once
            group = lax.rem(turn_no, 4) * 2 + turn_no // 4
            first = pl.multiple_of(group * LAT, LAT)
            firsts.append(first)
            wait_for(m_recv.at[pl.ds(first, LAT)], m_in.at[group])
        by_row = [
            jnp.transpose(m_recv[pl.ds(first, LAT)].astype(F32), (1, 0, 2)) for first in firsts
        ]
        block = by_row[0] if len(by_row) == 1 else jnp.concatenate(by_row, axis=1)

        def put(ref, lead, j, v):
            v = v.astype(BF16)
            for at_once, first in enumerate(firsts):
                ref[lead, pl.ds(first, LAT), j * LANES : (j + 1) * LANES] = v[at_once * LAT : (at_once + 1) * LAT]

        ends = block[12]
        us, yus, dus, xus, xds, yxds, dxus = [[[[None, None], [None, None]] for _ in range(2)] for _ in range(7)]
        for c in range(2):
            for s in range(2):
                v, up, down = [], [], []
                for k in range(3):
                    r = (c * 2 + s) * 3 + k
                    row = block[r]
                    v.append(row)
                    up.append(jnp.where(top16, turn(ends, r), turn(row, -1)))
                    down.append(jnp.where(bottom16, turn(ends, -r), turn(row, 1)))
                us[0][c][s], xus[0][c][s], xds[0][c][s] = v[1], v[2], v[0]
                yus[0][c][s], yxds[0][c][s] = up[1], up[0]
                dus[0][c][s], dxus[0][c][s] = down[1], down[2]
                us[1][c][s] = halves(v[2], v[0])
                crossed = turn(us[1][c][s], 64)
                xus[1][c][s] = halves(crossed, v[1])
                xds[1][c][s] = halves(v[1], crossed)
                yus[1][c][s] = halves(up[2], up[0])
                yxds[1][c][s] = halves(up[1], turn(up[2], 64))
                dus[1][c][s] = halves(down[2], down[0])
                dxus[1][c][s] = halves(turn(down[0], 64), down[1])
        for t in range(2):
            w = [jnp.broadcast_to(row_w[2 * j + t : 2 * j + t + 1, :], (BATCH, LANES)) for j in range(10)]
            out = site_speeds(us[t], yus[t], dus[t], xus[t], xds[t], yxds[t], dxus[t], w)
            for c in range(2):
                for s in range(2):
                    j = c * 4 + s * 2 + t
                    js = (j + 4) % 8
                    v = us[t][c][s]
                    put(right, 0, j, v)
                    put(right, 1, js, v if j >= 4 else -v)
                    for a in range(2):
                        put(left, a, j, out[a][s][c])

    for a in range(2):
        for c in range(2):
            prod = lax.dot_general(left[a], right[c], (((1,), (1,)), ((), ())), preferred_element_type=F32)
            part[:, 2 * a + c, :] = prod

    wait_for(e_recv, e_sem.at[1])
    f_send[...] = jnp.sum(e_recv[...], axis=0)
    for i in range(1, ST):
        remote(f_send, f_recv.at[st], f_sem.at[0], f_sem.at[1], lat, lax.rem(st + i, ST)).start()
    pltpu.make_async_copy(f_send, f_recv.at[st], f_sem.at[1]).start()

    for row, column in far:
        for c in range(2):
            p = row + c
            remote(part.at[p * ST + column], s_recv.at[me], s_sem.at[0], s_sem.at[1], p, column).start()
    remote(part.at[twin * ST + st], s_recv.at[me], s_sem.at[0], s_sem.at[1], twin, st).start()
    pltpu.make_async_copy(part.at[me], s_recv.at[me], s_sem.at[1]).start()

    wait_for(f_recv, f_sem.at[1])
    energies = jnp.sum(f_recv[...], axis=0)
    own = jnp.sum(jnp.where(lane == me, energies, 0.0), axis=1, keepdims=True)
    differ = own - energies
    weight = differ / (differ * differ + broaden * broaden)

    wait_for(s_recv, s_sem.at[1])

    sums = jnp.sum(s_recv[...], axis=0)
    velocity = sums * (1.0 / 256.0)
    both[0:4] = sums
    cross = velocity[1:2] * velocity[2:3] - velocity[0:1] * velocity[3:4]
    both[4:5] = jnp.broadcast_to(jnp.sum(weight * cross, axis=1, keepdims=True), (1, LANES))

    wait_for(c_recv.at[pl.ds(0, LAT // 2 - 1)], c_sem.at[0])
    wait_for(c_recv.at[pl.ds(0, LAT // 2)], d_sem.at[0])
    wait_for(r_recv.at[pl.ds(0, LAT - 1)], r_sem.at[0])
    wait_for(e_recv.at[pl.ds(0, LAT - 1)], e_sem.at[0])
    wait_for(f_recv.at[pl.ds(0, ST - 1)], f_sem.at[0])
    wait_for(m_recv.at[pl.ds(0, NDEV - 1)], m_out)
    wait_for(s_recv.at[pl.ds(0, NDEV - 1)], s_sem.at[0])


def rows_of(array):
    head = array.shape[:-2]
    array = array.reshape(head + (2, NH, LANES))
    return jnp.swapaxes(array, -3, -2).reshape(head + (2 * NH, LANES))


def local(raw_states, levels, phases, window):
    vm = pltpu.VMEM
    dma = pltpu.SemaphoreType.DMA
    scratch = [
        pltpu.SMEM((LAT,), jnp.int32),
        vm((3, 16, LANES), jnp.int32), vm((2, 16, LANES), jnp.int32),
        vm((5, 16, LANES), BF16), vm((LAT, 5, 16, LANES), BF16),
        vm((LAT, 2, 2, 16, LANES), BF16),
        vm((12, KX, 8, NH * LANES), F32), vm((2, KX, 8, NH * LANES), F32),
        vm((2, 2, 2, KX, 8, NH * LANES), F32), vm((2, 2, KX, 8, NH * LANES), F32),
        vm((2, 2, KX, 8, NH * LANES), F32),
        vm((24, LANES), F32), vm((2, KX, 8, NH * LANES), F32),
        vm((8, 2, ST, 16, LANES), BF16), vm((NDEV, 16, LANES), BF16),
        vm((2, NDEV, 1024), BF16), vm((2, NDEV, 1024), BF16),
        vm((NDEV, 4, LANES), F32), vm((NDEV, 4, LANES), F32),
        vm((1, LANES), F32), vm((LAT, 1, LANES), F32),
        vm((1, LANES), F32), vm((ST, 1, LANES), F32),
        dma((3,)), dma((2,)), dma((2,)), dma((LAT // 2,)), dma((2,)), dma, dma((ST,)), dma((2,)), dma((2,)), dma((2,)),
        pltpu.SemaphoreType.REGULAR((3,)),
    ]
    hbm = pl.BlockSpec(memory_space=pltpu.HBM)
    both = pl.pallas_call(
        kernel,
        out_shape=jax.ShapeDtypeStruct((8, LANES), F32),
        in_specs=[hbm] * 4,
        out_specs=pl.BlockSpec(memory_space=pltpu.VMEM),
        scratch_shapes=scratch,
        compiler_params=pltpu.CompilerParams(
            collective_id=0, has_side_effects=True, vmem_limit_bytes=50000000
        ),
    )(*(pltpu.with_memory_space_constraint(v, pltpu.HBM) for v in (rows_of(raw_states), rows_of(phases), rows_of(levels), window)))
    return both[:4].reshape(1, 2, 2, LANES) * (1.0 / 256.0), both[4, :1]


def solution(mesh):
    in_specs = (
        P(None, "st", None, "lat", None),
        P(None, "lat", None),
        P(None, "lat", None),
        P("st"),
    )
    out_specs = (P(("lat", "st"), None, None, None), P(("lat", "st")))
    return jax.shard_map(local, mesh=mesh, in_specs=in_specs, out_specs=out_specs, check_vma=False)
```

```python
import functools
import itertools
import math

import jax
import jax.numpy as jnp
from jax import lax
from jax.experimental import pallas as pl
from jax.experimental.pallas import tpu as pltpu
from jax.sharding import PartitionSpec as P

ORDER = 6
WINDOWS = 16
LEVELS = 8
PHASES = 8
F32 = jnp.float32
BF16 = jnp.bfloat16
MESH = pl.DeviceIdType.MESH

hop_far = 0.25
level_step = 0.3
stagger = 0.4
spectrum = 6.0
broaden = 0.2
angle_low = 0.5
angle_high = 2.6
half_root = 0.5 * math.sqrt(3.0)

unit = 2.0 / spectrum
LAT = 16
ST = 8
NDEV = LAT * ST
BATCH = 32
LANES = 128
KX = 4
NH = 8

ON_A, ON_B, C0, S0, C1, S1, C2X, S2X, C1Y, S1Y, C2Y, S2Y = range(12)


def y_up(v):
    return pltpu.roll(v, v.shape[1] - 1, 1)


def y_down(v):
    return pltpu.roll(v, 1, 1)


def x_up(get, k):
    return get(k + 1) if k < KX - 1 else pltpu.roll(get(0), 7, 0)


def x_down(get, k):
    return get(k - 1) if k > 0 else pltpu.roll(get(KX - 1), 1, 0)


def mul(cr, ci, ur, ui):
    return cr * ur - ci * ui, cr * ui + ci * ur


def mulc(cr, ci, ur, ui):
    return cr * ur + ci * ui, cr * ui - ci * ur


def eighth_cos(q):
    e = 2.0 - jnp.minimum(q, 8.0 - q)
    r = math.sqrt(0.5)
    cubic = (1.0 - 2.0 * r) / 6.0
    return e * ((r - cubic) + cubic * (e * e))


def build_coefs(numbers, co, c2):
    planes = [jnp.transpose(numbers[:, t].astype(F32), (1, 0, 2)) for t in range(5)]
    for k in range(KX):
        kk, e = k // 2, k % 2

        def plane(t):
            return jnp.concatenate([planes[t][2 * h + e, kk * 8 : kk * 8 + 8] for h in range(NH)], axis=1)

        for t, (cp, sp) in enumerate(((C0, S0), (C1, S1), (0, 1))):
            q = plane(t)
            cosq = (-1.0 / hop_far) * eighth_cos(q)
            qs = q + 6.0
            qs = jnp.where(qs >= 8.0, qs - 8.0, qs)
            sinq = (-1.0 / hop_far) * eighth_cos(qs)
            if t < 2:
                co[cp, k] = cosq
                co[sp, k] = sinq
            else:
                c2[0, k] = cosq
                c2[1, k] = sinq
            if t == 1:
                co[C1Y, k] = y_up(cosq)
                co[S1Y, k] = y_up(sinq)
            if t == 2:
                co[C2Y, k] = y_up(cosq)
                co[S2Y, k] = y_up(sinq)
        for t, dst, par in ((3, ON_A, 1.0), (4, ON_B, -1.0)):
            co[dst, k] = (1.0 / hop_far) * (level_step * (plane(t) - 0.5 * (LEVELS - 1)) + stagger * par)
    for k in range(KX):
        co[C2X, k] = x_down(lambda kk: c2[0, kk], k)
        co[S2X, k] = x_down(lambda kk: c2[1, kk], k)


def apply_h(get, co, k, before=None):
    u = [[get(c, s, k) for c in range(2)] for s in range(2)]
    up = [[x_up(functools.partial(get, c, s), k) for c in range(2)] for s in range(2)]
    dn = [[x_down(functools.partial(get, c, s), k) for c in range(2)] for s in range(2)]
    a = [[up[s][c] - u[s][c] for c in range(2)] for s in range(2)]
    b = before if before else [[u[s][c] - dn[s][c] for c in range(2)] for s in range(2)]
    near = mul(co[C0, k], co[S0, k], *u[1])
    r1 = mul(co[C1Y, k], co[S1Y, k], *u[1])
    r2 = mul(co[C2Y, k], co[S2Y, k], *up[1])
    on = co[ON_A, k]
    a_re = on * u[0][0] + near[0] - (a[0][1] + b[0][1]) + y_up(b[0][1]) + y_down(r1[0] + r2[0] + a[0][1])
    a_im = on * u[0][1] + near[1] + (a[0][0] + b[0][0]) - y_up(b[0][0]) + y_down(r1[1] + r2[1] - a[0][0])
    near = mulc(co[C0, k], co[S0, k], *u[0])
    q1 = mulc(co[C1, k], co[S1, k], *u[0])
    q2 = mulc(co[C2X, k], co[S2X, k], *dn[0])
    on = co[ON_B, k]
    b_re = on * u[1][0] + near[0] + (a[1][1] + b[1][1]) + y_up(q1[0] + q2[0] - b[1][1]) - y_down(a[1][1])
    b_im = on * u[1][1] + near[1] - (a[1][0] + b[1][0]) + y_up(q1[1] + q2[1] + b[1][0]) + y_down(a[1][0])
    return [[a_re, a_im], [b_re, b_im]], a


def site_speeds(u, yu, du, xu, xd, yxd, dxu, w):
    inv = hop_far
    hf = hop_far * half_root
    vf = hop_far * 1.5
    pick = lambda v, s: (v[0][s], v[1][s])
    out = [[None, None], [None, None]]
    for s, sign in ((0, 1.0), (1, -1.0)):
        other = 1 - s
        if s == 0:
            n0 = mul(w[0], w[1], *pick(u, other))
            one = mul(w[2], w[3], *pick(du, other))
            two = mul(w[4], w[5], *pick(dxu, other))
        else:
            n0 = mulc(w[0], w[1], *pick(u, other))
            one = mulc(w[6], w[7], *pick(yu, other))
            two = mulc(w[8], w[9], *pick(yxd, other))
        dif = [(sign * inv * half_root) * (one[c] - two[c]) for c in range(2)]
        tot = [(sign * inv) * (0.5 * (one[c] + two[c]) - n0[c]) for c in range(2)]
        far_x = [(yu[c][s] + yxd[c][s]) + (du[c][s] + dxu[c][s]) - 2.0 * (xu[c][s] + xd[c][s]) for c in range(2)]
        far_y = [(yu[c][s] - yxd[c][s]) + (du[c][s] - dxu[c][s]) for c in range(2)]
        out[0][s] = [dif[1] + (sign * hf) * far_x[0], (sign * hf) * far_x[1] - dif[0]]
        out[1][s] = [tot[1] + (sign * vf) * far_y[0], (sign * vf) * far_y[1] - tot[0]]
    return out


def hops(dyl, dz, dx, dyh):
    return (1 if dyl else 2 * dyh) + min(dz, 4 - dz) + min(dx, 4 - dx)


OFFSETS = sorted(itertools.product(range(2), range(4), range(4), range(2)), key=lambda d: (-hops(*d), d))


def columns_of_chips(lat):
    yl, z = lat // 8, lax.rem(lat // 2, 4)
    offsets = [(1, 2), (0, 2), (1, 1), (1, 3), (0, 1), (0, 3), (1, 0)]
    return [lax.rem(yl + a, 2) * 8 + lax.rem(z + b, 4) * 2 for a, b in offsets]


LAT_ORDER = [(1, 2), (0, 2), (1, 1), (1, 3), (0, 1), (0, 3), (1, 0), (0, 0)]
ST_ORDER = [(2, 1), (1, 1), (3, 1), (2, 0), (0, 1), (1, 0), (3, 0), (0, 0)]


def coordinates(lat, st):
    yl, z, x, yh = lat // 8, lax.rem(lat // 2, 4), st // 2, lax.rem(st, 2)
    rows = {(a, b): lax.rem(yl + a, 2) * 8 + lax.rem(z + b, 4) * 2 for a, b in LAT_ORDER}
    columns = {(a, b): lax.rem(x + a, 4) * 2 + lax.rem(yh + b, 2) for a, b in ST_ORDER}
    return rows, columns


def chips(lat, st):
    rows, columns = coordinates(lat, st)
    return [(rows[d[:2]], columns[d[2:]]) for d in OFFSETS if any(d)]


def kernel(
    raw, phases, levels, window, both,
    win_s, ph_v, lev_v, c_send, c_recv, r_recv, co, c2, field, total, low,
    row_w, tmp_w, m_send, m_recv, left, right, part, s_recv, e_send, e_recv, f_send, f_recv,
    in_sem, r_sem, c_sem, c_in, d_sem, m_out, m_in, s_sem, e_sem, f_sem, known,
):
    lat = lax.axis_index("lat")
    st = lax.axis_index("st")
    state = st * LAT + lat
    me = lat * ST + st
    slot = lax.rem(lat, 2) * 8 + lat // 2
    core = lax.rem(lat, 2)
    twin = lat + 1 - 2 * core

    def remote(src, dst, out_sem, in_sem, row, column):
        return pltpu.make_async_remote_copy(
            src, dst, out_sem, in_sem, device_id=(row, column), device_id_type=MESH
        )

    def wait_for(ref, sem):
        pltpu.make_async_copy(ref, ref, sem).wait()

    load_ph = pltpu.make_async_copy(phases, ph_v, in_sem.at[0])
    load_lev = pltpu.make_async_copy(levels, lev_v, in_sem.at[1])
    load_win = pltpu.make_async_copy(window, win_s, in_sem.at[2])
    load_ph.start()
    load_lev.start()
    load_win.start()
    near = columns_of_chips(lat)
    x, yh = st // 2, lax.rem(st, 2)
    along = [lax.rem(x + i, 4) * 2 + yh for i in (1, 3)]
    across = (lax.rem(lat + 8, LAT), st + 1 - 2 * yh)

    def greet(sem, row, column):
        pl.semaphore_signal(sem, inc=1, device_id=(row, column), device_id_type=MESH)

    barrier = pltpu.get_barrier_semaphore()
    for row in near:
        greet(barrier, row, st)
        greet(barrier, row + 1, st)
    for column in along:
        greet(barrier, lat, column)
    greet(barrier, *across)
    greet(barrier, twin, st)
    load_ph.wait()
    load_lev.wait()
    load_win.wait()
    c_send[0:3] = ph_v[...].astype(F32).astype(BF16)
    c_send[3:5] = lev_v[...].astype(F32).astype(BF16)
    pl.semaphore_wait(barrier, LAT - 1 + 3)

    mine = lat // 2
    for row in near:
        remote(c_send, c_recv.at[slot], c_sem.at[0], c_in.at[mine], row + core, st).start()
    remote(c_send, c_recv.at[slot], d_sem.at[0], d_sem.at[1], twin, st).start()
    pltpu.make_async_copy(c_send, c_recv.at[slot], c_sem.at[1]).start()
    for row in near:
        for c in range(2):
            remote(raw.at[:, row + c], r_recv.at[slot], r_sem.at[0], r_sem.at[1], row + c, st).start()
    remote(raw.at[:, twin], r_recv.at[slot], r_sem.at[0], r_sem.at[1], twin, st).start()
    pltpu.make_async_copy(raw.at[:, lat], r_recv.at[slot], r_sem.at[1]).start()
    for row in near:
        greet(known.at[0], row, st)
        greet(known.at[0], row + 1, st)
    greet(known.at[0], twin, st)

    w = angle_low + (angle_high - angle_low) * jnp.full((8, LANES), win_s[lat], jnp.int32).astype(F32) / (
        WINDOWS - 1
    )
    cosines = [jnp.ones((8, LANES), F32), jnp.cos(w)]
    for _ in range(2, ORDER + 1):
        cosines.append(2.0 * cosines[1] * cosines[-1] - cosines[-2])

    for row in reversed(near):
        row = row + core
        held = c_recv.at[core * 8 + row // 2]
        wait_for(held, c_in.at[row // 2])
        remote(held, held, d_sem.at[0], d_sem.at[1], twin, st).start()
    pl.semaphore_wait(known.at[0], LAT - 1)
    for column in along:
        greet(known.at[1], lat, column)
    wait_for(c_recv.at[slot], c_sem.at[1])
    wait_for(c_recv.at[pl.ds(0, LAT // 2)], d_sem.at[1])

    build_coefs(c_recv, co, c2)

    pl.semaphore_wait(known.at[1], 2)
    for column in along:
        greet(known.at[2], lat, column)
    wait_for(r_recv, r_sem.at[1])

    def wide(v):
        return jnp.concatenate([v] * NH, axis=1)

    coef = [wide(cosines[0])] + [wide(2.0 * v) for v in cosines[1:]]
    for c in range(2):
        for s in range(2):
            block = jnp.transpose(r_recv[:, c, s].astype(F32), (1, 0, 2))
            for k in range(KX):
                kk, e = k // 2, k % 2
                field[0, c, s, k] = jnp.concatenate(
                    [block[2 * h + e, kk * 8 : kk * 8 + 8] for h in range(NH)], axis=1
                )

    for degree in range(1, ORDER + 1):
        now, new = (degree - 1) % 2, degree % 2
        get = lambda c, s, k: field[now, c, s, k]
        step = None
        for k in range(KX):
            out, step = apply_h(get, co, k, step)
            for s in range(2):
                for c in range(2):
                    if degree == 1:
                        v = (0.5 * unit * hop_far) * out[s][c]
                        total[c, s, k] = field[0, c, s, k] + coef[1] * v
                    else:
                        v = (unit * hop_far) * out[s][c] - field[new, c, s, k]
                        psi = total[c, s, k] + coef[degree] * v
                        total[c, s, k] = psi
                        if degree == ORDER:
                            low[c, s, k] = psi.astype(BF16).astype(F32)
                    if degree < ORDER:
                        field[new, c, s, k] = v

    pl.semaphore_wait(known.at[2], 2)
    far = chips(lat, st)
    rows, columns = coordinates(lat, st)
    lane8 = lax.broadcasted_iota(jnp.int32, (8, LANES), 1)
    low8 = lane8 < 64
    half8 = lax.rem(lane8, 64)

    packed = [[None] * 12 for _ in range(2 * NH)]
    for c in range(2):
        for s in range(2):
            get = functools.partial(lambda c, s, k: low[c, s, k], c, s)
            column = {k: get(k) for k in range(KX)}
            column[-1] = x_down(get, 0)
            column[KX] = x_up(get, KX - 1)
            for i in range(3):
                for h in range(NH):
                    one = column[i - 1][:, h * LANES : (h + 1) * LANES]
                    two = column[i + 2][:, h * LANES : (h + 1) * LANES]
                    r = (c * 2 + s) * 3 + i
                    packed[2 * h][r] = jnp.where(low8, one, pltpu.roll(two, 64, 1))
                    packed[2 * h + 1][r] = jnp.where(low8, pltpu.roll(one, 64, 1), two)
    for j in range(2 * NH):
        after, before = packed[(j + 1) % 16], packed[j - 1]
        ends = [jnp.zeros((8, LANES), F32)] * 4
        for r in range(12):
            row, place = r % 4, r // 4
            up = pltpu.roll(after[r], 63 - place, 1)
            down = pltpu.roll(before[r], 65 + place, 1)
            ends[row] = jnp.where(half8 == 63 - place, up, jnp.where(half8 == place, down, ends[row]))
        rows16 = jnp.stack(packed[j] + ends, axis=0)
        m_send[:, j % 2, j // 2] = jnp.transpose(rows16, (1, 0, 2)).astype(BF16)

    for row, column in far:
        for c in range(2):
            p = row + c
            remote(m_send.at[p // 2, c, column], m_recv.at[state], m_out, m_in.at[st], p, column).start()
    remote(m_send.at[mine, 1 - core, st], m_recv.at[state], m_out, m_in.at[st], twin, st).start()
    pltpu.make_async_copy(m_send.at[mine, core, st], m_recv.at[state], m_in.at[st]).start()

    numer = jnp.zeros((8, NH * LANES), F32)
    denom = jnp.zeros((8, NH * LANES), F32)
    get = lambda c, s, k: total[c, s, k]
    step = None
    for k in range(KX):
        out, step = apply_h(get, co, k, step)
        for s in range(2):
            for c in range(2):
                v = total[c, s, k]
                numer = numer + v * out[s][c]
                denom = denom + v * v
    energy = jnp.sum(numer) / jnp.sum(denom) * hop_far
    lane = lax.broadcasted_iota(jnp.int32, (1, LANES), 1)
    e_send[...] = jnp.where(lane == state, jnp.full((1, LANES), energy, F32), 0.0)
    for i in range(1, LAT):
        remote(e_send, e_recv.at[lat], e_sem.at[0], e_sem.at[1], lax.rem(lat + i, LAT), st).start()
    pltpu.make_async_copy(e_send, e_recv.at[lat], e_sem.at[1]).start()

    line = lat // 2
    chunk = pl.ds(pl.multiple_of(st * LANES, LANES), LANES)
    low1 = lane < 64
    for j, plane in enumerate((C2X, S2X)):
        for k in range(KX):
            tmp_w[j, k] = y_up(co[plane, k])

    this_line = lax.broadcasted_iota(jnp.int32, (8, LANES), 0) == line

    def weight_row(j, k):
        if j in (4, 5):
            v = c2[j - 4, k, :, chunk]
        elif j in (8, 9):
            v = tmp_w[j - 8, k, :, chunk]
        else:
            v = co[(C0, S0, C1, S1, None, None, C1Y, S1Y)[j], k, :, chunk]
        return jnp.sum(jnp.where(this_line, v, 0.0), axis=0, keepdims=True)

    for j in range(10):
        rows = [weight_row(j, k) for k in range(KX)]
        swapped = [pltpu.roll(v, 64, 1) for v in rows]
        for t, (k1, k2) in enumerate(((0, 3), (1, 2))):
            first_half = jnp.where(low1, rows[k1], swapped[k2])
            second_half = jnp.where(low1, swapped[k1], rows[k2])
            row_w[2 * j + t : 2 * j + t + 1, :] = jnp.where(core == 0, first_half, second_half)

    lane16 = lax.broadcasted_iota(jnp.int32, (BATCH, LANES), 1)
    low16 = lane16 < 64
    top16 = lax.rem(lane16, 64) == 63
    bottom16 = lax.rem(lane16, 64) == 0

    def turn(v, by):
        return v if by % LANES == 0 else pltpu.roll(v, by % LANES, 1)

    def halves(one, two):
        return jnp.where(low16, one, two)

    @pl.loop(0, NDEV // BATCH)
    def _(i):
        firsts = []
        for at_once in range(BATCH // LAT):
            turn_no = i * (BATCH // LAT) + at_once
            group = lax.rem(turn_no, 4) * 2 + turn_no // 4
            first = pl.multiple_of(group * LAT, LAT)
            firsts.append(first)
            wait_for(m_recv.at[pl.ds(first, LAT)], m_in.at[group])
        by_row = [
            jnp.transpose(m_recv[pl.ds(first, LAT)].astype(F32), (1, 0, 2)) for first in firsts
        ]
        block = by_row[0] if len(by_row) == 1 else jnp.concatenate(by_row, axis=1)

        def put(ref, lead, j, v):
            v = v.astype(BF16)
            for at_once, first in enumerate(firsts):
                ref[lead, pl.ds(first, LAT), j * LANES : (j + 1) * LANES] = v[at_once * LAT : (at_once + 1) * LAT]

        ends = [block[12 + j] for j in range(4)]
        us, yus, dus, xus, xds, yxds, dxus = [[[[None, None], [None, None]] for _ in range(2)] for _ in range(7)]
        for c in range(2):
            for s in range(2):
                v, up, down = [], [], []
                for k in range(3):
                    r = (c * 2 + s) * 3 + k
                    row = block[r]
                    v.append(row)
                    up.append(jnp.where(top16, turn(ends[r % 4], r // 4), turn(row, -1)))
                    down.append(jnp.where(bottom16, turn(ends[r % 4], -(r // 4)), turn(row, 1)))
                us[0][c][s], xus[0][c][s], xds[0][c][s] = v[1], v[2], v[0]
                yus[0][c][s], yxds[0][c][s] = up[1], up[0]
                dus[0][c][s], dxus[0][c][s] = down[1], down[2]
                us[1][c][s] = halves(v[2], v[0])
                crossed = turn(us[1][c][s], 64)
                xus[1][c][s] = halves(crossed, v[1])
                xds[1][c][s] = halves(v[1], crossed)
                yus[1][c][s] = halves(up[2], up[0])
                yxds[1][c][s] = halves(up[1], turn(up[2], 64))
                dus[1][c][s] = halves(down[2], down[0])
                dxus[1][c][s] = halves(turn(down[0], 64), down[1])
        for t in range(2):
            w = [jnp.broadcast_to(row_w[2 * j + t : 2 * j + t + 1, :], (BATCH, LANES)) for j in range(10)]
            out = site_speeds(us[t], yus[t], dus[t], xus[t], xds[t], yxds[t], dxus[t], w)
            for c in range(2):
                for s in range(2):
                    j = c * 4 + s * 2 + t
                    js = (j + 4) % 8
                    v = us[t][c][s]
                    put(right, 0, j, v)
                    put(right, 1, js, v if j >= 4 else -v)
                    for a in range(2):
                        put(left, a, j, out[a][s][c])

    prods = [
        lax.dot_general(left[a], right[c], (((1,), (1,)), ((), ())), preferred_element_type=F32)
        for a in range(2)
        for c in range(2)
    ]
    part[...] = jnp.transpose(jnp.stack(prods, axis=0), (1, 0, 2))

    wait_for(e_recv, e_sem.at[1])
    f_send[...] = jnp.sum(e_recv[...], axis=0)
    for i in range(1, ST):
        remote(f_send, f_recv.at[st], f_sem.at[0], f_sem.at[1], lat, lax.rem(st + i, ST)).start()
    pltpu.make_async_copy(f_send, f_recv.at[st], f_sem.at[1]).start()

    for row, column in far:
        for c in range(2):
            p = row + c
            remote(part.at[p * ST + column], s_recv.at[me], s_sem.at[0], s_sem.at[1], p, column).start()
    remote(part.at[twin * ST + st], s_recv.at[me], s_sem.at[0], s_sem.at[1], twin, st).start()
    pltpu.make_async_copy(part.at[me], s_recv.at[me], s_sem.at[1]).start()

    wait_for(f_recv, f_sem.at[1])
    energies = jnp.sum(f_recv[...], axis=0)
    own = jnp.sum(jnp.where(lane == me, energies, 0.0), axis=1, keepdims=True)
    differ = own - energies
    weight = differ / (differ * differ + broaden * broaden)

    wait_for(s_recv, s_sem.at[1])

    sums = jnp.sum(s_recv[...], axis=0)
    velocity = sums * (1.0 / 256.0)
    both[0:4] = sums
    cross = velocity[1:2] * velocity[2:3] - velocity[0:1] * velocity[3:4]
    both[4:5] = jnp.broadcast_to(jnp.sum(weight * cross, axis=1, keepdims=True), (1, LANES))

    wait_for(c_recv.at[pl.ds(0, LAT // 2 - 1)], c_sem.at[0])
    wait_for(c_recv.at[pl.ds(0, LAT // 2)], d_sem.at[0])
    wait_for(r_recv.at[pl.ds(0, LAT - 1)], r_sem.at[0])
    wait_for(e_recv.at[pl.ds(0, LAT - 1)], e_sem.at[0])
    wait_for(f_recv.at[pl.ds(0, ST - 1)], f_sem.at[0])
    wait_for(m_recv.at[pl.ds(0, NDEV - 1)], m_out)
    wait_for(s_recv.at[pl.ds(0, NDEV - 1)], s_sem.at[0])


def rows_of(array):
    head = array.shape[:-2]
    array = array.reshape(head + (2, NH, LANES))
    return jnp.swapaxes(array, -3, -2).reshape(head + (2 * NH, LANES))


def local(raw_states, levels, phases, window):
    vm = pltpu.VMEM
    dma = pltpu.SemaphoreType.DMA
    scratch = [
        pltpu.SMEM((LAT,), jnp.int32),
        vm((3, 16, LANES), jnp.int32), vm((2, 16, LANES), jnp.int32),
        vm((5, 16, LANES), BF16), vm((LAT, 5, 16, LANES), BF16),
        vm((LAT, 2, 2, 16, LANES), BF16),
        vm((12, KX, 8, NH * LANES), F32), vm((2, KX, 8, NH * LANES), F32),
        vm((2, 2, 2, KX, 8, NH * LANES), F32), vm((2, 2, KX, 8, NH * LANES), F32),
        vm((2, 2, KX, 8, NH * LANES), F32),
        vm((24, LANES), F32), vm((2, KX, 8, NH * LANES), F32),
        vm((8, 2, ST, 16, LANES), BF16), vm((NDEV, 16, LANES), BF16),
        vm((2, NDEV, 1024), BF16), vm((2, NDEV, 1024), BF16),
        vm((NDEV, 4, LANES), F32), vm((NDEV, 4, LANES), F32),
        vm((1, LANES), F32), vm((LAT, 1, LANES), F32),
        vm((1, LANES), F32), vm((ST, 1, LANES), F32),
        dma((3,)), dma((2,)), dma((2,)), dma((LAT // 2,)), dma((2,)), dma, dma((ST,)), dma((2,)), dma((2,)), dma((2,)),
        pltpu.SemaphoreType.REGULAR((3,)),
    ]
    hbm = pl.BlockSpec(memory_space=pltpu.HBM)
    both = pl.pallas_call(
        kernel,
        out_shape=jax.ShapeDtypeStruct((8, LANES), F32),
        in_specs=[hbm] * 4,
        out_specs=pl.BlockSpec(memory_space=pltpu.VMEM),
        scratch_shapes=scratch,
        compiler_params=pltpu.CompilerParams(
            collective_id=0, has_side_effects=True, vmem_limit_bytes=50000000
        ),
    )(*(pltpu.with_memory_space_constraint(v, pltpu.HBM) for v in (rows_of(raw_states), rows_of(phases), rows_of(levels), window)))
    return both[:4].reshape(1, 2, 2, LANES) * (1.0 / 256.0), both[4, :1]


def solution(mesh):
    in_specs = (
        P(None, "st", None, "lat", None),
        P(None, "lat", None),
        P(None, "lat", None),
        P("st"),
    )
    out_specs = (P(("lat", "st"), None, None, None), P(("lat", "st")))
    return jax.shard_map(local, mesh=mesh, in_specs=in_specs, out_specs=out_specs, check_vma=False)
```

```python
import functools
import itertools
import math

import jax
import jax.numpy as jnp
from jax import lax
from jax.experimental import pallas as pl
from jax.experimental.pallas import tpu as pltpu
from jax.sharding import PartitionSpec as P

ORDER = 6
WINDOWS = 16
LEVELS = 8
PHASES = 8
F32 = jnp.float32
BF16 = jnp.bfloat16
MESH = pl.DeviceIdType.MESH

hop_far = 0.25
level_step = 0.3
stagger = 0.4
spectrum = 6.0
broaden = 0.2
angle_low = 0.5
angle_high = 2.6
half_root = 0.5 * math.sqrt(3.0)

unit = 2.0 / spectrum
LAT = 16
ST = 8
NDEV = LAT * ST
BATCH = 32
LANES = 128
KX = 4
NH = 8

ON_A, ON_B, C0, S0, C1, S1, C2X, S2X, C1Y, S1Y, C2Y, S2Y = range(12)


def y_up(v):
    return pltpu.roll(v, v.shape[1] - 1, 1)


def y_down(v):
    return pltpu.roll(v, 1, 1)


def x_up(get, k):
    return get(k + 1) if k < KX - 1 else pltpu.roll(get(0), 7, 0)


def x_down(get, k):
    return get(k - 1) if k > 0 else pltpu.roll(get(KX - 1), 1, 0)


def mul(cr, ci, ur, ui):
    return cr * ur - ci * ui, cr * ui + ci * ur


def mulc(cr, ci, ur, ui):
    return cr * ur + ci * ui, cr * ui - ci * ur


def eighth_cos(q):
    e = 2.0 - jnp.minimum(q, 8.0 - q)
    r = math.sqrt(0.5)
    cubic = (1.0 - 2.0 * r) / 6.0
    return e * ((r - cubic) + cubic * (e * e))


def build_coefs(numbers, co, c2):
    planes = [jnp.transpose(numbers[:, t].astype(F32), (1, 0, 2)) for t in range(5)]
    for k in range(KX):
        kk, e = k // 2, k % 2

        def plane(t):
            return jnp.concatenate([planes[t][2 * h + e, kk * 8 : kk * 8 + 8] for h in range(NH)], axis=1)

        for t, (cp, sp) in enumerate(((C0, S0), (C1, S1), (0, 1))):
            q = plane(t)
            cosq = (-1.0 / hop_far) * eighth_cos(q)
            qs = q + 6.0
            qs = jnp.where(qs >= 8.0, qs - 8.0, qs)
            sinq = (-1.0 / hop_far) * eighth_cos(qs)
            if t < 2:
                co[cp, k] = cosq
                co[sp, k] = sinq
            else:
                c2[0, k] = cosq
                c2[1, k] = sinq
            if t == 1:
                co[C1Y, k] = y_up(cosq)
                co[S1Y, k] = y_up(sinq)
            if t == 2:
                co[C2Y, k] = y_up(cosq)
                co[S2Y, k] = y_up(sinq)
        for t, dst, par in ((3, ON_A, 1.0), (4, ON_B, -1.0)):
            co[dst, k] = (1.0 / hop_far) * (level_step * (plane(t) - 0.5 * (LEVELS - 1)) + stagger * par)
    for k in range(KX):
        co[C2X, k] = x_down(lambda kk: c2[0, kk], k)
        co[S2X, k] = x_down(lambda kk: c2[1, kk], k)


def apply_h(get, co, k, before=None):
    u = [[get(c, s, k) for c in range(2)] for s in range(2)]
    up = [[x_up(functools.partial(get, c, s), k) for c in range(2)] for s in range(2)]
    dn = [[x_down(functools.partial(get, c, s), k) for c in range(2)] for s in range(2)]
    a = [[up[s][c] - u[s][c] for c in range(2)] for s in range(2)]
    b = before if before else [[u[s][c] - dn[s][c] for c in range(2)] for s in range(2)]
    near = mul(co[C0, k], co[S0, k], *u[1])
    r1 = mul(co[C1Y, k], co[S1Y, k], *u[1])
    r2 = mul(co[C2Y, k], co[S2Y, k], *up[1])
    on = co[ON_A, k]
    a_re = on * u[0][0] + near[0] - (a[0][1] + b[0][1]) + y_up(b[0][1]) + y_down(r1[0] + r2[0] + a[0][1])
    a_im = on * u[0][1] + near[1] + (a[0][0] + b[0][0]) - y_up(b[0][0]) + y_down(r1[1] + r2[1] - a[0][0])
    near = mulc(co[C0, k], co[S0, k], *u[0])
    q1 = mulc(co[C1, k], co[S1, k], *u[0])
    q2 = mulc(co[C2X, k], co[S2X, k], *dn[0])
    on = co[ON_B, k]
    b_re = on * u[1][0] + near[0] + (a[1][1] + b[1][1]) + y_up(q1[0] + q2[0] - b[1][1]) - y_down(a[1][1])
    b_im = on * u[1][1] + near[1] - (a[1][0] + b[1][0]) + y_up(q1[1] + q2[1] + b[1][0]) + y_down(a[1][0])
    return [[a_re, a_im], [b_re, b_im]], a


def site_speeds(u, yu, du, xu, xd, yxd, dxu, w):
    inv = hop_far
    hf = hop_far * half_root
    vf = hop_far * 1.5
    pick = lambda v, s: (v[0][s], v[1][s])
    out = [[None, None], [None, None]]
    for s, sign in ((0, 1.0), (1, -1.0)):
        other = 1 - s
        if s == 0:
            n0 = mul(w[0], w[1], *pick(u, other))
            one = mul(w[2], w[3], *pick(du, other))
            two = mul(w[4], w[5], *pick(dxu, other))
        else:
            n0 = mulc(w[0], w[1], *pick(u, other))
            one = mulc(w[6], w[7], *pick(yu, other))
            two = mulc(w[8], w[9], *pick(yxd, other))
        dif = [(sign * inv * half_root) * (one[c] - two[c]) for c in range(2)]
        tot = [(sign * inv) * (0.5 * (one[c] + two[c]) - n0[c]) for c in range(2)]
        far_x = [(yu[c][s] + yxd[c][s]) + (du[c][s] + dxu[c][s]) - 2.0 * (xu[c][s] + xd[c][s]) for c in range(2)]
        far_y = [(yu[c][s] - yxd[c][s]) + (du[c][s] - dxu[c][s]) for c in range(2)]
        out[0][s] = [dif[1] + (sign * hf) * far_x[0], (sign * hf) * far_x[1] - dif[0]]
        out[1][s] = [tot[1] + (sign * vf) * far_y[0], (sign * vf) * far_y[1] - tot[0]]
    return out


def hops(dyl, dz, dx, dyh):
    return (1 if dyl else 2 * dyh) + min(dz, 4 - dz) + min(dx, 4 - dx)


OFFSETS = sorted(itertools.product(range(2), range(4), range(4), range(2)), key=lambda d: (-hops(*d), d))


def columns_of_chips(lat):
    yl, z = lat // 8, lax.rem(lat // 2, 4)
    offsets = [(1, 2), (0, 2), (1, 1), (1, 3), (0, 1), (0, 3), (1, 0)]
    return [lax.rem(yl + a, 2) * 8 + lax.rem(z + b, 4) * 2 for a, b in offsets]


LAT_ORDER = [(1, 2), (0, 2), (1, 1), (1, 3), (0, 1), (0, 3), (1, 0), (0, 0)]
ST_ORDER = [(2, 1), (1, 1), (3, 1), (2, 0), (0, 1), (1, 0), (3, 0), (0, 0)]


def coordinates(lat, st):
    yl, z, x, yh = lat // 8, lax.rem(lat // 2, 4), st // 2, lax.rem(st, 2)
    rows = {(a, b): lax.rem(yl + a, 2) * 8 + lax.rem(z + b, 4) * 2 for a, b in LAT_ORDER}
    columns = {(a, b): lax.rem(x + a, 4) * 2 + lax.rem(yh + b, 2) for a, b in ST_ORDER}
    return rows, columns


def chips(lat, st):
    rows, columns = coordinates(lat, st)
    return [(rows[d[:2]], columns[d[2:]]) for d in OFFSETS if any(d)]


def kernel(
    raw, phases, levels, window, both,
    win_s, ph_v, lev_v, c_send, c_recv, r_recv, co, c2, field, total, low,
    row_w, tmp_w, m_send, m_recv, left, right, part, s_recv, e_send, e_recv, f_send, f_recv,
    in_sem, r_sem, c_sem, c_in, d_sem, m_out, m_in, s_sem, e_sem, f_sem, known,
):
    lat = lax.axis_index("lat")
    st = lax.axis_index("st")
    state = st * LAT + lat
    me = lat * ST + st
    slot = lax.rem(lat, 2) * 8 + lat // 2
    core = lax.rem(lat, 2)
    twin = lat + 1 - 2 * core

    def remote(src, dst, out_sem, in_sem, row, column):
        return pltpu.make_async_remote_copy(
            src, dst, out_sem, in_sem, device_id=(row, column), device_id_type=MESH
        )

    def wait_for(ref, sem):
        pltpu.make_async_copy(ref, ref, sem).wait()

    load_ph = pltpu.make_async_copy(phases, ph_v, in_sem.at[0])
    load_lev = pltpu.make_async_copy(levels, lev_v, in_sem.at[1])
    load_win = pltpu.make_async_copy(window, win_s, in_sem.at[2])
    load_ph.start()
    load_lev.start()
    load_win.start()
    near = columns_of_chips(lat)
    x, yh = st // 2, lax.rem(st, 2)
    along = [lax.rem(x + i, 4) * 2 + yh for i in (1, 3)]
    across = (lax.rem(lat + 8, LAT), st + 1 - 2 * yh)

    def greet(sem, row, column):
        pl.semaphore_signal(sem, inc=1, device_id=(row, column), device_id_type=MESH)

    barrier = pltpu.get_barrier_semaphore()
    for row in near:
        greet(barrier, row, st)
        greet(barrier, row + 1, st)
    for column in along:
        greet(barrier, lat, column)
    greet(barrier, *across)
    greet(barrier, twin, st)
    load_ph.wait()
    load_lev.wait()
    load_win.wait()
    c_send[0:3] = ph_v[...].astype(F32).astype(BF16)
    c_send[3:5] = lev_v[...].astype(F32).astype(BF16)
    pl.semaphore_wait(barrier, LAT - 1 + 3)

    mine = lat // 2
    for row in near:
        remote(c_send, c_recv.at[slot], c_sem.at[0], c_in.at[mine], row + core, st).start()
    remote(c_send, c_recv.at[slot], d_sem.at[0], d_sem.at[1], twin, st).start()
    pltpu.make_async_copy(c_send, c_recv.at[slot], c_sem.at[1]).start()
    for row in near:
        for c in range(2):
            remote(raw.at[:, row + c], r_recv.at[slot], r_sem.at[0], r_sem.at[1], row + c, st).start()
    remote(raw.at[:, twin], r_recv.at[slot], r_sem.at[0], r_sem.at[1], twin, st).start()
    pltpu.make_async_copy(raw.at[:, lat], r_recv.at[slot], r_sem.at[1]).start()
    for row in near:
        greet(known.at[0], row, st)
        greet(known.at[0], row + 1, st)
    greet(known.at[0], twin, st)

    w = angle_low + (angle_high - angle_low) * jnp.full((8, LANES), win_s[lat], jnp.int32).astype(F32) / (
        WINDOWS - 1
    )
    cosines = [jnp.ones((8, LANES), F32), jnp.cos(w)]
    for _ in range(2, ORDER + 1):
        cosines.append(2.0 * cosines[1] * cosines[-1] - cosines[-2])

    for row in reversed(near):
        row = row + core
        held = c_recv.at[core * 8 + row // 2]
        wait_for(held, c_in.at[row // 2])
        remote(held, held, d_sem.at[0], d_sem.at[1], twin, st).start()
    pl.semaphore_wait(known.at[0], LAT - 1)
    for column in along:
        greet(known.at[1], lat, column)
    wait_for(c_recv.at[slot], c_sem.at[1])
    wait_for(c_recv.at[pl.ds(0, LAT // 2)], d_sem.at[1])

    build_coefs(c_recv, co, c2)

    pl.semaphore_wait(known.at[1], 2)
    for column in along:
        greet(known.at[2], lat, column)
    wait_for(r_recv, r_sem.at[1])

    def wide(v):
        return jnp.concatenate([v] * NH, axis=1)

    coef = [wide(cosines[0])] + [wide(2.0 * v) for v in cosines[1:]]
    for c in range(2):
        for s in range(2):
            block = jnp.transpose(r_recv[:, c, s].astype(F32), (1, 0, 2))
            for k in range(KX):
                kk, e = k // 2, k % 2
                field[0, c, s, k] = jnp.concatenate(
                    [block[2 * h + e, kk * 8 : kk * 8 + 8] for h in range(NH)], axis=1
                )

    for degree in range(1, ORDER + 1):
        now, new = (degree - 1) % 2, degree % 2
        get = lambda c, s, k: field[now, c, s, k]
        step = None
        for k in range(KX):
            out, step = apply_h(get, co, k, step)
            for s in range(2):
                for c in range(2):
                    if degree == 1:
                        v = (0.5 * unit * hop_far) * out[s][c]
                        total[c, s, k] = field[0, c, s, k] + coef[1] * v
                    else:
                        v = (unit * hop_far) * out[s][c] - field[new, c, s, k]
                        psi = total[c, s, k] + coef[degree] * v
                        total[c, s, k] = psi
                        if degree == ORDER:
                            low[c, s, k] = psi.astype(BF16).astype(F32)
                    if degree < ORDER:
                        field[new, c, s, k] = v

    pl.semaphore_wait(known.at[2], 2)
    far = chips(lat, st)
    rows, columns = coordinates(lat, st)
    lane8 = lax.broadcasted_iota(jnp.int32, (8, LANES), 1)
    low8 = lane8 < 64
    half8 = lax.rem(lane8, 64)

    packed = [[None] * 12 for _ in range(2 * NH)]
    for c in range(2):
        for s in range(2):
            get = functools.partial(lambda c, s, k: low[c, s, k], c, s)
            column = {k: get(k) for k in range(KX)}
            column[-1] = x_down(get, 0)
            column[KX] = x_up(get, KX - 1)
            for i in range(3):
                for h in range(NH):
                    one = column[i - 1][:, h * LANES : (h + 1) * LANES]
                    two = column[i + 2][:, h * LANES : (h + 1) * LANES]
                    r = (c * 2 + s) * 3 + i
                    packed[2 * h][r] = jnp.where(low8, one, pltpu.roll(two, 64, 1))
                    packed[2 * h + 1][r] = jnp.where(low8, pltpu.roll(one, 64, 1), two)
    for j in range(2 * NH):
        after, before = packed[(j + 1) % 16], packed[j - 1]
        ends = [jnp.zeros((8, LANES), F32)] * 4
        for r in range(12):
            row, place = r % 4, r // 4
            up = pltpu.roll(after[r], 63 - place, 1)
            down = pltpu.roll(before[r], 65 + place, 1)
            ends[row] = jnp.where(half8 == 63 - place, up, jnp.where(half8 == place, down, ends[row]))
        rows16 = jnp.stack(packed[j] + ends, axis=0)
        m_send[:, j % 2, j // 2] = jnp.transpose(rows16, (1, 0, 2)).astype(BF16)

    for row, column in far:
        for c in range(2):
            p = row + c
            remote(m_send.at[p // 2, c, column], m_recv.at[state], m_out, m_in.at[st], p, column).start()
    remote(m_send.at[mine, 1 - core, st], m_recv.at[state], m_out, m_in.at[st], twin, st).start()
    pltpu.make_async_copy(m_send.at[mine, core, st], m_recv.at[state], m_in.at[st]).start()

    numer = jnp.zeros((8, NH * LANES), F32)
    denom = jnp.zeros((8, NH * LANES), F32)
    get = lambda c, s, k: total[c, s, k]
    step = None
    for k in range(KX):
        out, step = apply_h(get, co, k, step)
        for s in range(2):
            for c in range(2):
                v = total[c, s, k]
                numer = numer + v * out[s][c]
                denom = denom + v * v
    energy = jnp.sum(numer) / jnp.sum(denom) * hop_far
    lane = lax.broadcasted_iota(jnp.int32, (1, LANES), 1)
    e_send[...] = jnp.where(lane == state, jnp.full((1, LANES), energy, F32), 0.0)
    for i in range(1, LAT):
        remote(e_send, e_recv.at[lat], e_sem.at[0], e_sem.at[1], lax.rem(lat + i, LAT), st).start()
    pltpu.make_async_copy(e_send, e_recv.at[lat], e_sem.at[1]).start()

    line = lat // 2
    chunk = pl.ds(pl.multiple_of(st * LANES, LANES), LANES)
    low1 = lane < 64
    for j, plane in enumerate((C2X, S2X)):
        for k in range(KX):
            tmp_w[j, k] = y_up(co[plane, k])

    this_line = lax.broadcasted_iota(jnp.int32, (8, LANES), 0) == line

    def weight_row(j, k):
        if j in (4, 5):
            v = c2[j - 4, k, :, chunk]
        elif j in (8, 9):
            v = tmp_w[j - 8, k, :, chunk]
        else:
            v = co[(C0, S0, C1, S1, None, None, C1Y, S1Y)[j], k, :, chunk]
        return jnp.sum(jnp.where(this_line, v, 0.0), axis=0, keepdims=True)

    for j in range(10):
        rows = [weight_row(j, k) for k in range(KX)]
        swapped = [pltpu.roll(v, 64, 1) for v in rows]
        for t, (k1, k2) in enumerate(((0, 3), (1, 2))):
            first_half = jnp.where(low1, rows[k1], swapped[k2])
            second_half = jnp.where(low1, swapped[k1], rows[k2])
            row_w[2 * j + t : 2 * j + t + 1, :] = jnp.where(core == 0, first_half, second_half)

    lane16 = lax.broadcasted_iota(jnp.int32, (BATCH, LANES), 1)
    low16 = lane16 < 64
    top16 = lax.rem(lane16, 64) == 63
    bottom16 = lax.rem(lane16, 64) == 0

    def turn(v, by):
        return v if by % LANES == 0 else pltpu.roll(v, by % LANES, 1)

    def halves(one, two):
        return jnp.where(low16, one, two)

    @pl.loop(0, NDEV // BATCH)
    def _(i):
        firsts = []
        for at_once in range(BATCH // LAT):
            turn_no = i * (BATCH // LAT) + at_once
            group = lax.rem(st + turn_no, ST)
            first = pl.multiple_of(group * LAT, LAT)
            firsts.append(first)
            wait_for(m_recv.at[pl.ds(first, LAT)], m_in.at[group])
        by_row = [
            jnp.transpose(m_recv[pl.ds(first, LAT)].astype(F32), (1, 0, 2)) for first in firsts
        ]
        block = by_row[0] if len(by_row) == 1 else jnp.concatenate(by_row, axis=1)

        def put(ref, lead, j, v):
            v = v.astype(BF16)
            for at_once, first in enumerate(firsts):
                ref[lead, pl.ds(first, LAT), j * LANES : (j + 1) * LANES] = v[at_once * LAT : (at_once + 1) * LAT]

        ends = [block[12 + j] for j in range(4)]
        us, yus, dus, xus, xds, yxds, dxus = [[[[None, None], [None, None]] for _ in range(2)] for _ in range(7)]
        for c in range(2):
            for s in range(2):
                v, up, down = [], [], []
                for k in range(3):
                    r = (c * 2 + s) * 3 + k
                    row = block[r]
                    v.append(row)
                    up.append(jnp.where(top16, turn(ends[r % 4], r // 4), turn(row, -1)))
                    down.append(jnp.where(bottom16, turn(ends[r % 4], -(r // 4)), turn(row, 1)))
                us[0][c][s], xus[0][c][s], xds[0][c][s] = v[1], v[2], v[0]
                yus[0][c][s], yxds[0][c][s] = up[1], up[0]
                dus[0][c][s], dxus[0][c][s] = down[1], down[2]
                us[1][c][s] = halves(v[2], v[0])
                crossed = turn(us[1][c][s], 64)
                xus[1][c][s] = halves(crossed, v[1])
                xds[1][c][s] = halves(v[1], crossed)
                yus[1][c][s] = halves(up[2], up[0])
                yxds[1][c][s] = halves(up[1], turn(up[2], 64))
                dus[1][c][s] = halves(down[2], down[0])
                dxus[1][c][s] = halves(turn(down[0], 64), down[1])
        for t in range(2):
            w = [jnp.broadcast_to(row_w[2 * j + t : 2 * j + t + 1, :], (BATCH, LANES)) for j in range(10)]
            out = site_speeds(us[t], yus[t], dus[t], xus[t], xds[t], yxds[t], dxus[t], w)
            for c in range(2):
                for s in range(2):
                    j = c * 4 + s * 2 + t
                    js = (j + 4) % 8
                    v = us[t][c][s]
                    put(right, 0, j, v)
                    put(right, 1, js, v if j >= 4 else -v)
                    for a in range(2):
                        put(left, a, j, out[a][s][c])

    prods = [
        lax.dot_general(left[a], right[c], (((1,), (1,)), ((), ())), preferred_element_type=F32)
        for a in range(2)
        for c in range(2)
    ]
    part[...] = jnp.transpose(jnp.stack(prods, axis=0), (1, 0, 2))

    wait_for(e_recv, e_sem.at[1])
    f_send[...] = jnp.sum(e_recv[...], axis=0)
    for i in range(1, ST):
        remote(f_send, f_recv.at[st], f_sem.at[0], f_sem.at[1], lat, lax.rem(st + i, ST)).start()
    pltpu.make_async_copy(f_send, f_recv.at[st], f_sem.at[1]).start()

    for row, column in far:
        for c in range(2):
            p = row + c
            remote(part.at[p * ST + column], s_recv.at[me], s_sem.at[0], s_sem.at[1], p, column).start()
    remote(part.at[twin * ST + st], s_recv.at[me], s_sem.at[0], s_sem.at[1], twin, st).start()
    pltpu.make_async_copy(part.at[me], s_recv.at[me], s_sem.at[1]).start()

    wait_for(f_recv, f_sem.at[1])
    energies = jnp.sum(f_recv[...], axis=0)
    own = jnp.sum(jnp.where(lane == me, energies, 0.0), axis=1, keepdims=True)
    differ = own - energies
    weight = differ / (differ * differ + broaden * broaden)

    wait_for(s_recv, s_sem.at[1])

    sums = jnp.sum(s_recv[...], axis=0)
    velocity = sums * (1.0 / 256.0)
    both[0:4] = sums
    cross = velocity[1:2] * velocity[2:3] - velocity[0:1] * velocity[3:4]
    both[4:5] = jnp.broadcast_to(jnp.sum(weight * cross, axis=1, keepdims=True), (1, LANES))

    wait_for(c_recv.at[pl.ds(0, LAT // 2 - 1)], c_sem.at[0])
    wait_for(c_recv.at[pl.ds(0, LAT // 2)], d_sem.at[0])
    wait_for(r_recv.at[pl.ds(0, LAT - 1)], r_sem.at[0])
    wait_for(e_recv.at[pl.ds(0, LAT - 1)], e_sem.at[0])
    wait_for(f_recv.at[pl.ds(0, ST - 1)], f_sem.at[0])
    wait_for(m_recv.at[pl.ds(0, NDEV - 1)], m_out)
    wait_for(s_recv.at[pl.ds(0, NDEV - 1)], s_sem.at[0])


def rows_of(array):
    head = array.shape[:-2]
    array = array.reshape(head + (2, NH, LANES))
    return jnp.swapaxes(array, -3, -2).reshape(head + (2 * NH, LANES))


def local(raw_states, levels, phases, window):
    vm = pltpu.VMEM
    dma = pltpu.SemaphoreType.DMA
    scratch = [
        pltpu.SMEM((LAT,), jnp.int32),
        vm((3, 16, LANES), jnp.int32), vm((2, 16, LANES), jnp.int32),
        vm((5, 16, LANES), BF16), vm((LAT, 5, 16, LANES), BF16),
        vm((LAT, 2, 2, 16, LANES), BF16),
        vm((12, KX, 8, NH * LANES), F32), vm((2, KX, 8, NH * LANES), F32),
        vm((2, 2, 2, KX, 8, NH * LANES), F32), vm((2, 2, KX, 8, NH * LANES), F32),
        vm((2, 2, KX, 8, NH * LANES), F32),
        vm((24, LANES), F32), vm((2, KX, 8, NH * LANES), F32),
        vm((8, 2, ST, 16, LANES), BF16), vm((NDEV, 16, LANES), BF16),
        vm((2, NDEV, 1024), BF16), vm((2, NDEV, 1024), BF16),
        vm((NDEV, 4, LANES), F32), vm((NDEV, 4, LANES), F32),
        vm((1, LANES), F32), vm((LAT, 1, LANES), F32),
        vm((1, LANES), F32), vm((ST, 1, LANES), F32),
        dma((3,)), dma((2,)), dma((2,)), dma((LAT // 2,)), dma((2,)), dma, dma((ST,)), dma((2,)), dma((2,)), dma((2,)),
        pltpu.SemaphoreType.REGULAR((3,)),
    ]
    hbm = pl.BlockSpec(memory_space=pltpu.HBM)
    both = pl.pallas_call(
        kernel,
        out_shape=jax.ShapeDtypeStruct((8, LANES), F32),
        in_specs=[hbm] * 4,
        out_specs=pl.BlockSpec(memory_space=pltpu.VMEM),
        scratch_shapes=scratch,
        compiler_params=pltpu.CompilerParams(
            collective_id=0, has_side_effects=True, vmem_limit_bytes=50000000
        ),
    )(*(pltpu.with_memory_space_constraint(v, pltpu.HBM) for v in (rows_of(raw_states), rows_of(phases), rows_of(levels), window)))
    return both[:4].reshape(1, 2, 2, LANES) * (1.0 / 256.0), both[4, :1]


def solution(mesh):
    in_specs = (
        P(None, "st", None, "lat", None),
        P(None, "lat", None),
        P(None, "lat", None),
        P("st"),
    )
    out_specs = (P(("lat", "st"), None, None, None), P(("lat", "st")))
    return jax.shard_map(local, mesh=mesh, in_specs=in_specs, out_specs=out_specs, check_vma=False)
```
